1024 devices in a mesh: depth: 32 (over z), rows: 32 (over x, y, core).
Axes of the slice: x: 4, y: 4, z: 32, core: 2. Of those that a mesh axis runs over, the one named last changes fastest.
Arguments:
- fuel: float32 [128, 256, 512], P('depth', 'rows'), may hold values from -6 to 6
- heat: float32 [128, 256, 512], P('depth', 'rows'), may hold values from -6 to 6
- kappa: float32 [128, 256, 512], P('depth', 'rows'), may hold values from 0.02 to 0.15
- vel_z: float32 [128, 256, 512], P('depth', 'rows'), may hold values from -0.4 to 0.4
- vel_y: float32 [128, 256, 512], P('depth', 'rows'), may hold values from -0.4 to 0.4
- tf_centre: float32 [8], replicated, may hold values from -1.5 to 1.5
- tf_width: float32 [8], replicated, may hold values from 0.4 to 1.5
- tf_density: float32 [8], replicated, may hold values from 0.5 to 4
- tf_tint: float32 [8, 3], replicated, may hold values from -2 to 2
Outputs:
- picture: float32 [8, 4, 256, 512], P(None, None, 'rows', 'depth')
The draws below stay inside these ranges and needn't reach their ends.
All inputs are finite; a program needn't handle non-finite values.
Results may differ from the reference program's by a relative error of at most 0.000022.
Values sent between devices are 32-bit elements; how exact they have to be, the bound alone decides.
No kernel may reach another device: no remote copies, remote signals or barrier semaphores. Data moves between devices by JAX's collectives and lax.ppermute only.
A program may use at most 32 MiB of HBM per device.

```python
import math
import jax
import jax.numpy as jnp
from jax import lax

X = 512
NTF = 8
NZ = 128
NY = 256


def steps_of(own_key, shape, split, least, high):
    loudness = 1.0
    for dim, blocks in split:
        steps = jax.random.uniform(jax.random.fold_in(jax.random.fold_in(own_key, 6), dim), (blocks,), jnp.float32, least / len(split), high / len(split))
        loudness = loudness * jnp.repeat(jnp.exp(steps), shape[dim] // blocks).reshape((-1,) + (1,) * (len(shape) - 1 - dim))
    return loudness


def bell_draw(own_key, extent, spread, bound, shards=(), dtype=jnp.bfloat16):
    drawn = jax.random.normal(own_key, extent, jnp.float32) * spread
    if len(shards) > 0:
        drawn = steps_of(own_key, extent, shards, -0.22, 0.18) * drawn
    return jnp.clip(drawn, min=-bound, max=bound).astype(dtype)


def setup_inputs(seed: int = 0) -> dict:
    keys = jax.random.split(jax.random.key(seed), 10)
    fuel = bell_draw(keys[0], (NZ, NY, X), 1.0, 6.0, ((0, 32), (1, 32)), jnp.float32)
    heat = bell_draw(keys[1], (NZ, NY, X), 1.0, 6.0, ((0, 32), (1, 32)), jnp.float32)
    kappa = jnp.clip(jnp.exp(math.log(0.15) - 2.014903 * jax.random.uniform(keys[2], (NZ, NY, X), jnp.float32) ** steps_of(keys[2], (NZ, NY, X), ((0, 32), (1, 32)), -0.2, 0.2)), 0.02, 0.15)
    vel_z = jnp.clip(jax.random.uniform(keys[3], (NZ, NY, X), jnp.float32, -0.4, 0.4) * steps_of(keys[3], (NZ, NY, X), ((0, 32), (1, 32)), -0.4, 0.0), -0.4, 0.4)
    vel_y = jnp.clip(jax.random.uniform(keys[4], (NZ, NY, X), jnp.float32, -0.4, 0.4) * steps_of(keys[4], (NZ, NY, X), ((0, 32), (1, 32)), -0.4, 0.0), -0.4, 0.4)
    tf_centre = jnp.clip(jax.random.uniform(keys[5], (NTF,), jnp.float32, -1.5, 1.5), -1.5, 1.5)
    tf_width = jnp.clip(jnp.exp(jax.random.uniform(keys[6], (NTF,), jnp.float32, math.log(0.4), math.log(1.5))), 0.4, 1.5)
    tf_density = jnp.clip(jnp.exp(jax.random.uniform(keys[7], (NTF,), jnp.float32, math.log(0.5), math.log(4.0))), 0.5, 4.0)
    tf_tint = jnp.clip(jax.random.uniform(keys[8], (NTF, 3), jnp.float32, -2.0, 2.0), -2.0, 2.0)
    return {"fuel": fuel, "heat": heat, "kappa": kappa, "vel_z": vel_z, "vel_y": vel_y, "tf_centre": tf_centre, "tf_width": tf_width, "tf_density": tf_density, "tf_tint": tf_tint}


time_step = 1.0
lewis_ratio = 0.8
heat_release = 0.6
burn_rate = 0.5

def stencil_parts(field, vel_z, vel_y):
    padded = jnp.pad(field, ((0, 0), (0, 0), (1, 1)))
    centre = padded[1:-1, 1:-1, 1:-1]
    neighbours = padded[2:, 1:-1, 1:-1] + padded[:-2, 1:-1, 1:-1]
    neighbours = neighbours + padded[1:-1, 2:, 1:-1] + padded[1:-1, :-2, 1:-1]
    neighbours = neighbours + padded[1:-1, 1:-1, 2:] + padded[1:-1, 1:-1, :-2]
    transport = vel_z * (padded[2:, 1:-1, 1:-1] - padded[:-2, 1:-1, 1:-1]) * 0.5
    transport = transport + vel_y * (padded[1:-1, 2:, 1:-1] - padded[1:-1, :-2, 1:-1]) * 0.5
    return (centre, neighbours - 6.0 * centre, transport)

def tendency(fuel_wide, heat_wide, kappa, vel_z, vel_y):
    fuel_mid, fuel_lap, fuel_adv = stencil_parts(fuel_wide, vel_z, vel_y)
    heat_mid, heat_lap, heat_adv = stencil_parts(heat_wide, vel_z, vel_y)
    burning = burn_rate * fuel_mid * heat_mid * heat_mid / (1.0 + heat_mid * heat_mid)
    return (lewis_ratio * kappa * fuel_lap - fuel_adv - burning, kappa * heat_lap - heat_adv + heat_release * burning)

def shading(framed):
    padded = jnp.pad(framed, ((0, 0), (0, 0), (1, 1)))
    grad_z = (padded[2:, 1:-1, 1:-1] - padded[:-2, 1:-1, 1:-1]) * 0.5
    grad_y = (padded[1:-1, 2:, 1:-1] - padded[1:-1, :-2, 1:-1]) * 0.5
    grad_x = (padded[1:-1, 1:-1, 2:] - padded[1:-1, 1:-1, :-2]) * 0.5
    norm_sq = grad_z * grad_z + grad_y * grad_y + grad_x * grad_x + 1.0
    facing = (0.48 * grad_z + 0.6 * grad_y + 0.64 * grad_x) / jnp.sqrt(norm_sq)
    return 0.35 + 0.65 * facing * facing

def march(level, fuel_now, lighting, tf_centre, tf_width, tf_density, tf_tint, opacity_scale):
    functions = tf_centre.shape[0]
    start_state = (jnp.zeros((functions, 3) + level.shape[1:], jnp.float32), jnp.ones((functions,) + level.shape[1:], jnp.float32))

    def plane(state_pair, plane_data):
        colour, passing = state_pair
        level_plane, fuel_plane, light_plane = plane_data
        offset = (level_plane[None] - tf_centre[:, None, None]) / tf_width[:, None, None]
        extinct = tf_density[:, None, None] * jnp.exp(-offset * offset) * opacity_scale
        survive = jnp.exp(-extinct)
        tinted = jax.nn.sigmoid(tf_tint[:, :, None, None] * fuel_plane[None, None])
        emitted = ((1.0 - survive) * light_plane[None])[:, None] * tinted
        return ((colour + passing[:, None] * emitted, passing * survive), None)
    (colour, passing), unused = lax.scan(plane, start_state, (level, fuel_now, lighting))
    return (colour, passing)

def bordered(field):
    return jnp.pad(field, ((1, 1), (1, 1), (0, 0)))

def reference(fuel, heat, kappa, vel_z, vel_y, tf_centre, tf_width, tf_density, tf_tint):
    rate_u, rate_v = tendency(bordered(fuel), bordered(heat), kappa, vel_z, vel_y)
    first_u = fuel + time_step * rate_u
    first_v = heat + time_step * rate_v
    rate_u, rate_v = tendency(bordered(first_u), bordered(first_v), kappa, vel_z, vel_y)
    final_u = 0.5 * (fuel + first_u + time_step * rate_u)
    final_v = 0.5 * (heat + first_v + time_step * rate_v)
    lighting = shading(bordered(final_v))
    colour, passing = march(final_v, final_u, lighting, tf_centre, tf_width, tf_density, tf_tint, 4.0 / NZ)
    return jnp.concatenate([colour, passing[:, None]], axis=1)
```

```python
import functools

import jax
import jax.numpy as jnp
from jax import lax
from jax.experimental import pallas as pl
from jax.experimental.pallas import tpu as pltpu
from jax.sharding import PartitionSpec as P

time_step = 1.0
lewis_ratio = 0.8
heat_release = 0.6
burn_rate = 0.5

WF = 3
WC = 2

vmem = pl.BlockSpec(memory_space=pltpu.VMEM)
smem = pl.BlockSpec(memory_space=pltpu.SMEM)


def pairs(axis):
    count = lax.axis_size(axis)
    forward = [(i, i + 1) for i in range(count - 1)]
    return forward, [(target, source) for source, target in forward]


def exchange(to_next, to_prev, axis):
    forward, backward = pairs(axis)
    return lax.ppermute(to_next, axis, forward), lax.ppermute(to_prev, axis, backward)


def planes_kernel(fuel, heat, kappa, vel_z, vel_y, to_next, to_prev):
    planes = fuel.shape[0]
    at = 0
    for field, width in ((fuel, WF), (heat, WF), (kappa, WC), (vel_z, WC), (vel_y, WC)):
        to_next[at : at + width] = field[planes - width : planes]
        to_prev[at : at + width] = field[0:width]
        at += width


def deep_planes(fields, low, high):
    planes = fields[0].shape[0]
    at = 0
    columns = []
    for field, width in zip(fields, (WF, WF, WC, WC, WC)):
        column = [(low, at + i) for i in range(width)]
        column += [(field, i) for i in range(planes)]
        column += [(high, at + i) for i in range(width)]
        columns.append((column, width))
        at += width
    return columns


def rows_kernel(fuel, heat, kappa, vel_z, vel_y, low, high, to_next, to_prev):
    rows = fuel.shape[1]
    at = 0
    for column, width in deep_planes((fuel, heat, kappa, vel_z, vel_y), low, high):
        for source, i in column:
            to_next[at : at + width] = source[i, rows - width : rows]
            to_prev[at : at + width] = source[i, 0:width]
            at += width


def side(value, step):
    size = value.shape[1]
    lane = lax.broadcasted_iota(jnp.int32, value.shape, 1)
    if step > 0:
        return jnp.where(lane < size - 1, pltpu.roll(value, size - 1, 1), 0.0)
    return jnp.where(lane > 0, pltpu.roll(value, 1, 1), 0.0)


def above(value):
    return pltpu.roll(value, value.shape[0] - 1, 0)


def below(value):
    return pltpu.roll(value, 1, 0)


def parts(ref, i, vel_z, vel_y):
    centre = ref[i]
    ahead, behind = ref[i + 1], ref[i - 1]
    up, down = above(centre), below(centre)
    near = (ahead + behind) + (up + down) + (side(centre, 1) + side(centre, -1))
    transport = 0.5 * (vel_z * (ahead - behind) + vel_y * (up - down))
    return centre, near - 6.0 * centre, transport


def rates(fuel_ref, heat_ref, i, kappa, vel_z, vel_y, both):
    heat_mid, heat_lap, heat_adv = parts(heat_ref, i, vel_z, vel_y)
    square = heat_mid * heat_mid
    if both:
        fuel_mid, fuel_lap, fuel_adv = parts(fuel_ref, i, vel_z, vel_y)
    else:
        fuel_mid = fuel_ref[i]
    burning = burn_rate * fuel_mid * square / (1.0 + square)
    rate_heat = kappa * heat_lap - heat_adv + heat_release * burning
    if not both:
        return None, rate_heat
    return lewis_ratio * kappa * fuel_lap - fuel_adv - burning, rate_heat


def block_transpose(tile):
    row = lax.broadcasted_iota(jnp.int32, tile.shape, 0)
    block = lax.broadcasted_iota(jnp.int32, tile.shape, 1) // 16
    for bit in (1, 2, 4):
        later = pltpu.roll(pltpu.roll(tile, 8 - bit, 0), 16 * bit, 1)
        earlier = pltpu.roll(pltpu.roll(tile, bit, 0), 128 - 16 * bit, 1)
        row_bit, block_bit = (row & bit) != 0, (block & bit) != 0
        swapped = jnp.where(block_bit, later, earlier)
        tile = jnp.where(row_bit == block_bit, tile, swapped)
    return tile


def step_kernel(
    fuel, heat, kappa, vel_z, vel_y, low, high, row_low, row_high, out,
    fuel_s, heat_s, kappa_s, vel_z_s, vel_y_s, fuel_one, heat_one, heat_two, fuel_two,
):
    planes, rows = fuel.shape[0], fuel.shape[1]
    own = slice(WF, WF + rows)
    at = 0
    whole = (fuel_s, heat_s, kappa_s, vel_z_s, vel_y_s)
    columns = deep_planes((fuel, heat, kappa, vel_z, vel_y), low, high)
    for target, (column, width) in zip(whole, columns):
        for j, (source, i) in enumerate(column):
            target[j, own] = source[i]
            target[j, WF - width : WF] = row_low[at : at + width]
            target[j, WF + rows : WF + rows + width] = row_high[at : at + width]
            at += width

    def first(j, carry):
        rate_fuel, rate_heat = rates(
            fuel_s, heat_s, j + 1, kappa_s[j], vel_z_s[j], vel_y_s[j], True
        )
        fuel_one[j] = fuel_s[j + 1] + time_step * rate_fuel
        heat_one[j] = heat_s[j + 1] + time_step * rate_heat
        return carry

    lax.fori_loop(0, planes + 4, first, 0)

    def second(j, both):
        rate_fuel, rate_heat = rates(
            fuel_one, heat_one, j + 1, kappa_s[j + 1], vel_z_s[j + 1], vel_y_s[j + 1], both
        )
        heat_two[j] = 0.5 * (heat_s[j + 2] + heat_one[j + 1] + time_step * rate_heat)
        if both:
            fuel_two[j] = 0.5 * (fuel_s[j + 2] + fuel_one[j + 1] + time_step * rate_fuel)

    def inner(j, carry):
        second(j, True)
        return carry

    second(0, False)
    lax.fori_loop(1, planes + 1, inner, 0)
    second(planes + 1, False)

    groups = fuel.shape[2] // 128

    def shade(p):
        centre = heat_two[p + 1]
        grad_z = (heat_two[p + 2] - heat_two[p]) * 0.5
        grad_y = (above(centre) - below(centre)) * 0.5
        grad_x = (side(centre, 1) - side(centre, -1)) * 0.5
        norm_sq = grad_z * grad_z + grad_y * grad_y + grad_x * grad_x + 1.0
        facing = 0.48 * grad_z + 0.6 * grad_y + 0.64 * grad_x
        return 0.35 + 0.65 * (facing * facing) / norm_sq

    for p in range(planes):
        light = shade(p)
        for f, value in enumerate((heat_two[p + 1], fuel_two[p + 1], light)):
            value = value[own]
            lanes = slice((f * planes + p) * 128, (f * planes + p + 1) * 128)
            for m in range(groups):
                tile = block_transpose(value[:, m * 128 : (m + 1) * 128])
                for l in range(8):
                    out[8 * m + l, :, lanes] = tile[l : l + 1]


def per_function(ref, *index):
    row = lax.broadcasted_iota(jnp.int32, (8, 128), 0)
    value = jnp.full((8, 128), ref[(0,) + index], jnp.float32)
    for k in range(1, 8):
        value = jnp.where(row == k, ref[(k,) + index], value)
    return value


def march_kernel(opacity_scale, planes, centre, width, density, tint, fields, out):
    mid = per_function(centre)
    inverse = 1.0 / per_function(width)
    thick = per_function(density) * opacity_scale
    half = [0.5 * per_function(tint, c) for c in range(3)]

    def segment(s, state):
        passing, colour = state[0], list(state[1:])
        for p in range(planes):
            level, fuel, light = (
                fields[s, :, (f * planes + p) * 128 : (f * planes + p + 1) * 128]
                for f in range(3)
            )
            offset = (level - mid) * inverse
            survive = jnp.exp(-thick * jnp.exp(-offset * offset))
            weight = passing * (1.0 - survive) * (0.5 * light)
            for c in range(3):
                colour[c] = colour[c] + weight * (1.0 + jnp.tanh(half[c] * fuel))
            passing = passing * survive
        return (passing, *colour)

    zero = jnp.zeros((8, 128), jnp.float32)
    state = lax.fori_loop(0, fields.shape[0], segment, (zero + 1.0, zero, zero, zero))
    for c, value in enumerate((state[1], state[2], state[3], state[0])):
        tile = block_transpose(value)
        for k in range(8):
            out[k, c] = tile[:, 16 * k : 16 * k + 16]


def body(fuel, heat, kappa, vel_z, vel_y, tf_centre, tf_width, tf_density, tf_tint):
    planes, rows, columns = fuel.shape
    depth_count = lax.axis_size("depth")
    fields = (fuel, heat, kappa, vel_z, vel_y)
    f32 = functools.partial(jax.ShapeDtypeStruct, dtype=jnp.float32)
    sent_planes = 2 * WF + 3 * WC
    sent_rows = 2 * WF * (planes + 2 * WF) + 3 * WC * (planes + 2 * WC)

    to_next, to_prev = pl.pallas_call(
        planes_kernel,
        out_shape=[f32((sent_planes, rows, columns))] * 2,
        in_specs=[vmem] * 5,
        out_specs=[vmem] * 2,
        name="pack_planes",
    )(*fields)
    low, high = exchange(to_next, to_prev, "depth")
    to_next, to_prev = pl.pallas_call(
        rows_kernel,
        out_shape=[f32((sent_rows, columns))] * 2,
        in_specs=[vmem] * 7,
        out_specs=[vmem] * 2,
        name="pack_rows",
    )(*fields, low, high)
    row_low, row_high = exchange(to_next, to_prev, "rows")

    tall = rows + 8
    segment = f32((depth_count, 1, 3 * planes * 128))
    scratch = [pltpu.VMEM((planes + 2 * w, tall, columns), jnp.float32) for w in (WF, WF, WC, WC, WC)]
    scratch += [pltpu.VMEM((planes + 4, tall, columns), jnp.float32)] * 2
    scratch += [pltpu.VMEM((planes + 2, tall, columns), jnp.float32)] * 2
    stepped = pl.pallas_call(
        step_kernel,
        out_shape=segment,
        in_specs=[vmem] * 9,
        out_specs=vmem,
        scratch_shapes=scratch,
        name="step",
    )(*fields, low, high, row_low, row_high)

    gathered = lax.all_to_all(stepped, "depth", split_axis=0, concat_axis=0, tiled=True)

    return pl.pallas_call(
        functools.partial(march_kernel, 4.0 / (planes * depth_count), planes),
        out_shape=f32((8, 4, rows, columns // depth_count)),
        in_specs=[smem] * 4 + [vmem],
        out_specs=vmem,
        name="march",
    )(tf_centre, tf_width, tf_density, tf_tint, gathered)


def solution(mesh):
    placed = (P("depth", "rows", None),) * 5 + (P(),) * 4
    return jax.shard_map(
        body, mesh=mesh, in_specs=placed, out_specs=P(None, None, "rows", "depth"), check_vma=False
    )
```

```python
import functools

import jax
import jax.numpy as jnp
from jax import lax
from jax.experimental import pallas as pl
from jax.experimental.pallas import tpu as pltpu
from jax.sharding import PartitionSpec as P

time_step = 1.0
lewis_ratio = 0.8
heat_release = 0.6
burn_rate = 0.5

DF = 2
DC = 1
WF = 3
depths = (DF, DF, DC, DC, DC)

vmem = pl.BlockSpec(memory_space=pltpu.VMEM)
smem = pl.BlockSpec(memory_space=pltpu.SMEM)


def pairs(axis):
    count = lax.axis_size(axis)
    forward = [(i, i + 1) for i in range(count - 1)]
    return forward, [(target, source) for source, target in forward]


def exchange(to_next, to_prev, axis):
    forward, backward = pairs(axis)
    return lax.ppermute(to_next, axis, forward), lax.ppermute(to_prev, axis, backward)


def params(**more):
    return pltpu.CompilerParams(vmem_limit_bytes=8 << 20, **more)


def planes_kernel(fuel, heat, kappa, vel_z, vel_y, to_next, to_prev):
    planes = fuel.shape[0]
    at = 0
    for field, width in zip((fuel, heat, kappa, vel_z, vel_y), depths):
        to_next[at : at + width] = field[planes - width : planes]
        to_prev[at : at + width] = field[0:width]
        at += width


def deep_planes(fields, low, high):
    planes = fields[0].shape[0]
    at = 0
    columns = []
    for field, deep in zip(fields, depths):
        column = [(low, at + i, 1 + i) for i in range(deep)]
        column += [(field, i, 1 + deep) for i in range(planes)]
        column += [(high, at + i, deep - i) for i in range(deep)]
        columns.append(column)
        at += deep
    return columns


def rows_kernel(fuel, heat, kappa, vel_z, vel_y, low, high, to_next, to_prev):
    rows = fuel.shape[1]
    at = 0
    for column in deep_planes((fuel, heat, kappa, vel_z, vel_y), low, high):
        for source, i, width in column:
            to_next[at : at + width] = source[i, rows - width : rows]
            to_prev[at : at + width] = source[i, 0:width]
            at += width


def side(value, step):
    size = value.shape[1]
    lane = lax.broadcasted_iota(jnp.int32, value.shape, 1)
    if step > 0:
        return jnp.where(lane < size - 1, pltpu.roll(value, size - 1, 1), 0.0)
    return jnp.where(lane > 0, pltpu.roll(value, 1, 1), 0.0)


def above(value):
    return pltpu.roll(value, value.shape[0] - 1, 0)


def below(value):
    return pltpu.roll(value, 1, 0)


def parts(ref, i, vel_z, vel_y):
    centre = ref[i]
    ahead, behind = ref[i + 1], ref[i - 1]
    up, down = above(centre), below(centre)
    near = (ahead + behind) + (up + down) + (side(centre, 1) + side(centre, -1))
    transport = 0.5 * (vel_z * (ahead - behind) + vel_y * (up - down))
    return centre, near - 6.0 * centre, transport


def rates(fuel_ref, heat_ref, i, kappa, vel_z, vel_y):
    fuel_mid, fuel_lap, fuel_adv = parts(fuel_ref, i, vel_z, vel_y)
    heat_mid, heat_lap, heat_adv = parts(heat_ref, i, vel_z, vel_y)
    square = heat_mid * heat_mid
    burning = burn_rate * fuel_mid * square / (1.0 + square)
    return (
        lewis_ratio * kappa * fuel_lap - fuel_adv - burning,
        kappa * heat_lap - heat_adv + heat_release * burning,
    )


def block_transpose(tile):
    row = lax.broadcasted_iota(jnp.int32, tile.shape, 0)
    block = lax.broadcasted_iota(jnp.int32, tile.shape, 1) // 16
    for bit in (1, 2, 4):
        later = pltpu.roll(pltpu.roll(tile, 8 - bit, 0), 16 * bit, 1)
        earlier = pltpu.roll(pltpu.roll(tile, bit, 0), 128 - 16 * bit, 1)
        row_bit, block_bit = (row & bit) != 0, (block & bit) != 0
        swapped = jnp.where(block_bit, later, earlier)
        tile = jnp.where(row_bit == block_bit, tile, swapped)
    return tile


def step_kernel(
    fuel, heat, kappa, vel_z, vel_y, low, high, row_low, row_high, out,
    fuel_s, heat_s, kappa_s, vel_z_s, vel_y_s, fuel_one, heat_one, heat_two, fuel_two, edge,
):
    planes, rows, size = fuel.shape
    own = slice(WF, WF + rows)
    at = 0
    whole = (fuel_s, heat_s, kappa_s, vel_z_s, vel_y_s)
    columns = deep_planes((fuel, heat, kappa, vel_z, vel_y), low, high)
    for target, column in zip(whole, columns):
        for j, (source, i, width) in enumerate(column):
            target[j, own] = source[i]
            target[j, WF - width : WF] = row_low[at : at + width]
            target[j, WF + rows : WF + rows + width] = row_high[at : at + width]
            at += width

    def first(j, carry):
        rate_fuel, rate_heat = rates(
            fuel_s, heat_s, j + 1, kappa_s[j], vel_z_s[j], vel_y_s[j]
        )
        fuel_one[j] = fuel_s[j + 1] + time_step * rate_fuel
        heat_one[j] = heat_s[j + 1] + time_step * rate_heat
        return carry

    lax.fori_loop(0, planes + 2, first, 0)

    def second(j, carry):
        rate_fuel, rate_heat = rates(
            fuel_one, heat_one, j + 1, kappa_s[j + 1], vel_z_s[j + 1], vel_y_s[j + 1]
        )
        fuel_two[j] = 0.5 * (fuel_s[j + 2] + fuel_one[j + 1] + time_step * rate_fuel)
        heat_two[j] = 0.5 * (heat_s[j + 2] + heat_one[j + 1] + time_step * rate_heat)
        return carry

    lax.fori_loop(0, planes, second, 0)

    def send(value, at):
        lanes = slice(at * 128, (at + 1) * 128)
        for m in range(size // 128):
            tile = block_transpose(value[:, m * 128 : (m + 1) * 128])
            for l in range(8):
                out[8 * m + l, :, lanes] = tile[l : l + 1]

    lane = lax.broadcasted_iota(jnp.int32, (rows, size), 1)
    place = lane % 16
    borders = jnp.zeros((rows, size), jnp.float32)
    for p in range(planes):
        level = heat_two[p, own]
        send(level, p)
        send(fuel_two[p, own], planes + p)
        edge[p : p + 1] = heat_two[p, WF - 1 : WF]
        edge[planes + p : planes + p + 1] = heat_two[p, WF + rows : WF + rows + 1]
        left = (place == p) & (lane >= 16)
        right = (place == planes + p) & (lane < size - 16)
        borders = jnp.where(left, pltpu.roll(level, p + 1, 1), borders)
        borders = jnp.where(right, pltpu.roll(level, size - 16 + planes + p, 1), borders)
    send(edge[...], 2 * planes)
    send(borders, 2 * planes + 1)


def per_function(ref, *index):
    row = lax.broadcasted_iota(jnp.int32, (8, 128), 0)
    value = jnp.full((8, 128), ref[(0,) + index], jnp.float32)
    for k in range(1, 8):
        value = jnp.where(row == k, ref[(k,) + index], value)
    return value


def shift_rows(value, step):
    size = value.shape[0]
    row = lax.broadcasted_iota(jnp.int32, value.shape, 0)
    if step > 0:
        return jnp.where(row < size - 1, pltpu.roll(value, size - 1, 0), 0.0)
    return jnp.where(row > 0, pltpu.roll(value, 1, 0), 0.0)


def march_kernel(opacity_scale, planes, centre, width, density, tint, fields, out, lights):
    count = fields.shape[0]
    columns = [fields[:, 0, i * 128 : (i + 1) * 128] for i in range(planes)]
    edge, borders = (
        fields[:, 0, i * 128 : (i + 1) * 128] for i in (2 * planes, 2 * planes + 1)
    )
    lane = lax.broadcasted_iota(jnp.int32, (count, 128), 1)
    place = lane % 16
    for p in range(planes):
        level = columns[p]
        ahead = columns[p + 1] if p + 1 < planes else shift_rows(columns[0], 1)
        behind = columns[p - 1] if p > 0 else shift_rows(columns[planes - 1], -1)

        def moved(value, by):
            by = by % 128
            return pltpu.roll(value, by, 1) if by else value

        up = jnp.where(lane < 112, moved(level, -16), moved(edge, 112 - 16 * (planes + p)))
        down = jnp.where(lane >= 16, moved(level, 16), moved(edge, -16 * p))
        right = jnp.where(place < 15, moved(level, -1), moved(borders, 15 - planes - p))
        left = jnp.where(place > 0, moved(level, 1), moved(borders, -p))
        grad_z, grad_y, grad_x = 0.5 * (ahead - behind), 0.5 * (up - down), 0.5 * (right - left)
        norm_sq = grad_z * grad_z + grad_y * grad_y + grad_x * grad_x + 1.0
        facing = 0.48 * grad_z + 0.6 * grad_y + 0.64 * grad_x
        lights[p] = 0.5 * (0.35 + 0.65 * (facing * facing) / norm_sq)

    mid = per_function(centre)
    inverse = 1.0 / per_function(width)
    thick = per_function(density) * opacity_scale
    half = [0.5 * per_function(tint, c) for c in range(3)]

    def segment(s, state):
        passing, colour = state[0], list(state[1:])
        for p in range(planes):
            level = fields[s, :, p * 128 : (p + 1) * 128]
            fuel = fields[s, :, (planes + p) * 128 : (planes + p + 1) * 128]
            light = lights[p, pl.ds(s, 1)]
            offset = (level - mid) * inverse
            survive = jnp.exp(-thick * jnp.exp(-offset * offset))
            weight = passing * (1.0 - survive) * light
            for c in range(3):
                colour[c] = colour[c] + weight * (1.0 + jnp.tanh(half[c] * fuel))
            passing = passing * survive
        return (passing, *colour)

    zero = jnp.zeros((8, 128), jnp.float32)
    state = lax.fori_loop(0, count, segment, (zero + 1.0, zero, zero, zero))
    for c, value in enumerate((state[1], state[2], state[3], state[0])):
        tile = block_transpose(value)
        for k in range(8):
            out[k, c] = tile[:, 16 * k : 16 * k + 16]


def body(fuel, heat, kappa, vel_z, vel_y, tf_centre, tf_width, tf_density, tf_tint):
    planes, rows, columns = fuel.shape
    depth_count = lax.axis_size("depth")
    fields = (fuel, heat, kappa, vel_z, vel_y)
    f32 = functools.partial(jax.ShapeDtypeStruct, dtype=jnp.float32)
    sent_planes = sum(depths)
    sent_rows = sum(planes * (1 + deep) + deep * (1 + deep) for deep in depths)

    to_next, to_prev = pl.pallas_call(
        planes_kernel,
        out_shape=[f32((sent_planes, rows, columns))] * 2,
        in_specs=[vmem] * 5,
        out_specs=[vmem] * 2,
        compiler_params=params(),
        name="pack_planes",
    )(*fields)
    low, high = exchange(to_next, to_prev, "depth")
    to_next, to_prev = pl.pallas_call(
        rows_kernel,
        out_shape=[f32((sent_rows, columns))] * 2,
        in_specs=[vmem] * 7,
        out_specs=[vmem] * 2,
        compiler_params=params(),
        name="pack_rows",
    )(*fields, low, high)
    row_low, row_high = exchange(to_next, to_prev, "rows")

    tall = rows + 8
    segment = f32((depth_count, 1, (2 * planes + 2) * 128))
    scratch = [pltpu.VMEM((planes + 2 * deep, tall, columns), jnp.float32) for deep in depths]
    scratch += [pltpu.VMEM((planes + 2, tall, columns), jnp.float32)] * 2
    scratch += [pltpu.VMEM((planes, tall, columns), jnp.float32)] * 2
    scratch += [pltpu.VMEM((2 * planes, columns), jnp.float32)]
    stepped = pl.pallas_call(
        step_kernel,
        out_shape=segment,
        in_specs=[vmem] * 9,
        out_specs=vmem,
        scratch_shapes=scratch,
        compiler_params=params(),
        name="step",
    )(*fields, low, high, row_low, row_high)

    gathered = lax.all_to_all(stepped, "depth", split_axis=0, concat_axis=0, tiled=True)

    return pl.pallas_call(
        functools.partial(march_kernel, 4.0 / (planes * depth_count), planes),
        out_shape=f32((8, 4, rows, columns // depth_count)),
        in_specs=[smem] * 4 + [vmem],
        out_specs=vmem,
        scratch_shapes=[pltpu.VMEM((planes, depth_count, 128), jnp.float32)],
        compiler_params=params(),
        name="march",
    )(tf_centre, tf_width, tf_density, tf_tint, gathered)


def solution(mesh):
    placed = (P("depth", "rows", None),) * 5 + (P(),) * 4
    return jax.shard_map(
        body, mesh=mesh, in_specs=placed, out_specs=P(None, None, "rows", "depth"), check_vma=False
    )
```

```python
import functools
import math

import jax
import jax.numpy as jnp
from jax import lax
from jax.experimental import pallas as pl
from jax.experimental.pallas import tpu as pltpu
from jax.sharding import PartitionSpec as P

time_step = 1.0
lewis_ratio = 0.8
heat_release = 0.6
burn_rate = 0.5

depths = (2, 2, 1, 1, 1)
log2_e = math.log2(math.e)

vmem = pl.BlockSpec(memory_space=pltpu.VMEM)
smem = pl.BlockSpec(memory_space=pltpu.SMEM)
hbm = pl.BlockSpec(memory_space=pltpu.HBM)


def pairs(axis):
    count = lax.axis_size(axis)
    forward = [(i, i + 1) for i in range(count - 1)]
    return forward, [(target, source) for source, target in forward]


def exchange(to_next, to_prev, axis):
    forward, backward = pairs(axis)
    return lax.ppermute(to_next, axis, forward), lax.ppermute(to_prev, axis, backward)


def params(**more):
    return pltpu.CompilerParams(vmem_limit_bytes=8 << 20, **more)


def planes_kernel(fuel, heat, kappa, vel_z, vel_y, to_next, to_prev, arrived):
    planes = fuel.shape[0]
    at, copies = 0, []
    for field, deep in zip((fuel, heat, kappa, vel_z, vel_y), depths):
        for source, target in ((planes - deep, to_next), (0, to_prev)):
            copies.append(
                pltpu.make_async_copy(
                    field.at[pl.ds(source, deep)],
                    target.at[pl.ds(at, deep)],
                    arrived.at[len(copies)],
                )
            )
        at += deep
    for copy in copies:
        copy.start()
    for copy in copies:
        copy.wait()


def deep_planes(fields, low, high):
    planes = fields[0].shape[0]
    at = 0
    columns = []
    for field, deep in zip(fields, depths):
        column = [(low, at + i, 1 + i) for i in range(deep)]
        column += [(field, i, 1 + deep) for i in range(planes)]
        column += [(high, at + i, deep - i) for i in range(deep)]
        columns.append(column)
        at += deep
    return columns


def rows_kernel(fuel, heat, kappa, vel_z, vel_y, low, high, to_next, to_prev):
    rows = fuel.shape[1]
    at = 0
    for column in deep_planes((fuel, heat, kappa, vel_z, vel_y), low, high):
        for source, i, width in column:
            to_next[at : at + width] = source[i, rows - width : rows]
            to_prev[at : at + width] = source[i, 0:width]
            at += width


def side(value, step):
    size = value.shape[1]
    lane = lax.broadcasted_iota(jnp.int32, value.shape, 1)
    if step > 0:
        return jnp.where(lane < size - 1, pltpu.roll(value, size - 1, 1), 0.0)
    return jnp.where(lane > 0, pltpu.roll(value, 1, 1), 0.0)


def above(value):
    return pltpu.roll(value, value.shape[0] - 1, 0)


def below(value):
    return pltpu.roll(value, 1, 0)


def parts(ref, i, vel_z, vel_y):
    centre = ref[i]
    ahead, behind = ref[i + 1], ref[i - 1]
    up, down = above(centre), below(centre)
    near = (ahead + behind) + (up + down) + (side(centre, 1) + side(centre, -1))
    transport = 0.5 * (vel_z * (ahead - behind) + vel_y * (up - down))
    return centre, near - 6.0 * centre, transport


def rates(fuel_ref, heat_ref, i, kappa, vel_z, vel_y):
    fuel_mid, fuel_lap, fuel_adv = parts(fuel_ref, i, vel_z, vel_y)
    heat_mid, heat_lap, heat_adv = parts(heat_ref, i, vel_z, vel_y)
    square = heat_mid * heat_mid
    burning = burn_rate * fuel_mid * square / (1.0 + square)
    return (
        lewis_ratio * kappa * fuel_lap - fuel_adv - burning,
        kappa * heat_lap - heat_adv + heat_release * burning,
    )


def block_transpose(tile):
    row = lax.broadcasted_iota(jnp.int32, tile.shape, 0)
    block = lax.broadcasted_iota(jnp.int32, tile.shape, 1) // 16
    for bit in (1, 2, 4):
        later = pltpu.roll(pltpu.roll(tile, 8 - bit, 0), 16 * bit, 1)
        earlier = pltpu.roll(pltpu.roll(tile, bit, 0), 128 - 16 * bit, 1)
        row_bit, block_bit = (row & bit) != 0, (block & bit) != 0
        swapped = jnp.where(block_bit, later, earlier)
        tile = jnp.where(row_bit == block_bit, tile, swapped)
    return tile


def step_kernel(
    fuel, heat, kappa, vel_z, vel_y, low, high, row_low, row_high, out,
    fuel_s, heat_s, kappa_s, vel_z_s, vel_y_s, fuel_one, heat_one, heat_two, fuel_two, edge,
):
    planes, rows, size = fuel.shape
    tall = fuel_s.shape[1]
    own = slice(0, rows)
    at = 0
    whole = (fuel_s, heat_s, kappa_s, vel_z_s, vel_y_s)
    columns = deep_planes((fuel, heat, kappa, vel_z, vel_y), low, high)
    for target, column in zip(whole, columns):
        for j, (source, i, width) in enumerate(column):
            target[j, own] = source[i]
            target[j, tall - width : tall] = row_low[at : at + width]
            target[j, rows : rows + width] = row_high[at : at + width]
            at += width

    def first(j, carry):
        rate_fuel, rate_heat = rates(
            fuel_s, heat_s, j + 1, kappa_s[j], vel_z_s[j], vel_y_s[j]
        )
        fuel_one[j] = fuel_s[j + 1] + time_step * rate_fuel
        heat_one[j] = heat_s[j + 1] + time_step * rate_heat
        return carry

    lax.fori_loop(0, planes + 2, first, 0)

    def second(j, carry):
        rate_fuel, rate_heat = rates(
            fuel_one, heat_one, j + 1, kappa_s[j + 1], vel_z_s[j + 1], vel_y_s[j + 1]
        )
        fuel_two[j] = 0.5 * (fuel_s[j + 2] + fuel_one[j + 1] + time_step * rate_fuel)
        heat_two[j] = 0.5 * (heat_s[j + 2] + heat_one[j + 1] + time_step * rate_heat)
        return carry

    lax.fori_loop(0, planes, second, 0)

    chunk = 2 * planes + 2

    def send(value, at):
        for m in range(size // 128):
            tile = block_transpose(value[:, m * 128 : (m + 1) * 128])
            out[pl.ds(8 * m * chunk + at, 8, stride=chunk), :] = tile

    lane = lax.broadcasted_iota(jnp.int32, (rows, size), 1)
    place = lane % 16
    borders = jnp.zeros((rows, size), jnp.float32)
    for p in range(planes):
        level = heat_two[p, own]
        send(level, p)
        send(fuel_two[p, own], planes + p)
        edge[p : p + 1] = heat_two[p, tall - 1 : tall]
        edge[planes + p : planes + p + 1] = heat_two[p, rows : rows + 1]
        left = (place == p) & (lane >= 16)
        right = (place == planes + p) & (lane < size - 16)
        borders = jnp.where(left, pltpu.roll(level, p + 1, 1), borders)
        borders = jnp.where(right, pltpu.roll(level, size - 16 + planes + p, 1), borders)
    send(edge[...], 2 * planes)
    send(borders, 2 * planes + 1)


def per_function(ref, *index):
    row = lax.broadcasted_iota(jnp.int32, (8, 128), 0)
    value = jnp.full((8, 128), ref[(0,) + index], jnp.float32)
    for k in range(1, 8):
        value = jnp.where(row == k, ref[(k,) + index], value)
    return value


def shift_rows(value, step):
    size = value.shape[0]
    row = lax.broadcasted_iota(jnp.int32, value.shape, 0)
    if step > 0:
        return jnp.where(row < size - 1, pltpu.roll(value, size - 1, 0), 0.0)
    return jnp.where(row > 0, pltpu.roll(value, 1, 0), 0.0)


def march_kernel(opacity_scale, planes, centre, width, density, tint, fields, out, lights):
    chunk = 2 * planes + 2
    count = fields.shape[0] // chunk
    columns = [fields[pl.ds(i, count, stride=chunk), :] for i in range(planes)]
    edge, borders = (
        fields[pl.ds(2 * planes + i, count, stride=chunk), :] for i in range(2)
    )
    lane = lax.broadcasted_iota(jnp.int32, (count, 128), 1)
    place = lane % 16
    for p in range(planes):
        level = columns[p]
        ahead = columns[p + 1] if p + 1 < planes else shift_rows(columns[0], 1)
        behind = columns[p - 1] if p > 0 else shift_rows(columns[planes - 1], -1)

        def moved(value, by):
            by = by % 128
            return pltpu.roll(value, by, 1) if by else value

        up = jnp.where(lane < 112, moved(level, -16), moved(edge, 112 - 16 * (planes + p)))
        down = jnp.where(lane >= 16, moved(level, 16), moved(edge, -16 * p))
        right = jnp.where(place < 15, moved(level, -1), moved(borders, 15 - planes - p))
        left = jnp.where(place > 0, moved(level, 1), moved(borders, -p))
        grad_z, grad_y, grad_x = 0.5 * (ahead - behind), 0.5 * (up - down), 0.5 * (right - left)
        norm_sq = grad_z * grad_z + grad_y * grad_y + grad_x * grad_x + 1.0
        facing = 0.48 * grad_z + 0.6 * grad_y + 0.64 * grad_x
        lights[p] = 0.5 * (0.35 + 0.65 * (facing * facing) / norm_sq)

    mid = per_function(centre)
    spread = per_function(width)
    narrow = -log2_e / (spread * spread)
    thick = per_function(density) * (-log2_e * opacity_scale)
    half = [0.5 * per_function(tint, c) for c in range(3)]

    def one_plane(s, p, state):
        passing, total, *colour = state
        at = s * chunk + p
        level, fuel = fields[pl.ds(at, 1), :], fields[pl.ds(at + planes, 1), :]
        offset = level - mid
        survive = jnp.exp2(thick * jnp.exp2(narrow * (offset * offset)))
        weight = passing * (1.0 - survive) * lights[p, pl.ds(s, 1)]
        colour = [value + weight * jnp.tanh(half[c] * fuel) for c, value in enumerate(colour)]
        return (passing * survive, total + weight, *colour)

    joint = 4

    def segments(i, state):
        for s in range(joint):
            for p in range(planes):
                state = one_plane(i * joint + s, p, state)
        return state

    zero = jnp.zeros((8, 128), jnp.float32)
    state = lax.fori_loop(0, count // joint, segments, (zero + 1.0, zero, zero, zero, zero))
    passing, total, *colour = state
    for c, value in enumerate([total + value for value in colour] + [passing]):
        tile = block_transpose(value)
        for k in range(8):
            out[k, c] = tile[:, 16 * k : 16 * k + 16]


def body(fuel, heat, kappa, vel_z, vel_y, tf_centre, tf_width, tf_density, tf_tint):
    planes, rows, columns = fuel.shape
    depth_count = lax.axis_size("depth")
    fields = (fuel, heat, kappa, vel_z, vel_y)
    f32 = functools.partial(jax.ShapeDtypeStruct, dtype=jnp.float32)
    sent_planes = sum(depths)
    sent_rows = sum(planes * (1 + deep) + deep * (1 + deep) for deep in depths)

    to_next, to_prev = pl.pallas_call(
        planes_kernel,
        out_shape=[f32((sent_planes, rows, columns))] * 2,
        in_specs=[hbm] * 5,
        out_specs=[vmem] * 2,
        scratch_shapes=[pltpu.SemaphoreType.DMA((2 * len(depths),))],
        compiler_params=params(),
        name="pack_planes",
    )(*(pltpu.with_memory_space_constraint(field, pltpu.HBM) for field in fields))
    low, high = exchange(to_next, to_prev, "depth")
    to_next, to_prev = pl.pallas_call(
        rows_kernel,
        out_shape=[f32((sent_rows, columns))] * 2,
        in_specs=[vmem] * 7,
        out_specs=[vmem] * 2,
        compiler_params=params(),
        name="pack_rows",
    )(*fields, low, high)
    row_low, row_high = exchange(to_next, to_prev, "rows")

    tall = rows + 8
    chunk = 2 * planes + 2
    scratch = [pltpu.VMEM((planes + 2 * deep, tall, columns), jnp.float32) for deep in depths]
    scratch += [pltpu.VMEM((planes + 2, tall, columns), jnp.float32)] * 2
    scratch += [pltpu.VMEM((planes, tall, columns), jnp.float32)] * 2
    scratch += [pltpu.VMEM((2 * planes, columns), jnp.float32)]
    stepped = pl.pallas_call(
        step_kernel,
        out_shape=f32((depth_count * chunk, 128)),
        in_specs=[vmem] * 9,
        out_specs=vmem,
        scratch_shapes=scratch,
        compiler_params=params(),
        name="step",
    )(*fields, low, high, row_low, row_high)

    gathered = lax.all_to_all(
        stepped.reshape(depth_count, 1, chunk * 128), "depth", split_axis=0, concat_axis=0, tiled=True
    ).reshape(depth_count * chunk, 128)

    return pl.pallas_call(
        functools.partial(march_kernel, 4.0 / (planes * depth_count), planes),
        out_shape=f32((8, 4, rows, columns // depth_count)),
        in_specs=[smem] * 4 + [vmem],
        out_specs=vmem,
        scratch_shapes=[pltpu.VMEM((planes, depth_count, 128), jnp.float32)],
        compiler_params=params(),
        name="march",
    )(tf_centre, tf_width, tf_density, tf_tint, gathered)


def solution(mesh):
    placed = (P("depth", "rows", None),) * 5 + (P(),) * 4
    return jax.shard_map(
        body, mesh=mesh, in_specs=placed, out_specs=P(None, None, "rows", "depth"), check_vma=False
    )
```

```python
import functools
import math

import jax
import jax.numpy as jnp
from jax import lax
from jax.experimental import pallas as pl
from jax.experimental.pallas import tpu as pltpu
from jax.sharding import PartitionSpec as P

time_step = 1.0
lewis_ratio = 0.8
heat_release = 0.6
burn_rate = 0.5

depths = (2, 2, 1, 1, 1)
log2_e = math.log2(math.e)

vmem = pl.BlockSpec(memory_space=pltpu.VMEM)
smem = pl.BlockSpec(memory_space=pltpu.SMEM)
hbm = pl.BlockSpec(memory_space=pltpu.HBM)


def first_member(count):
    return 5 * count // 8


def pairs(axis):
    count = lax.axis_size(axis)
    forward = [(i, i + 1) for i in range(count - 1)]
    return forward, [(target, source) for source, target in forward]


def exchange(to_next, to_prev, axis):
    forward, backward = pairs(axis)
    return lax.ppermute(to_next, axis, forward), lax.ppermute(to_prev, axis, backward)


def params(**more):
    return pltpu.CompilerParams(vmem_limit_bytes=8 << 20, **more)


def planes_kernel(fuel, heat, kappa, vel_z, vel_y, to_next, to_prev, arrived):
    planes = fuel.shape[0]
    at, copies = 0, []
    for field, deep in zip((fuel, heat, kappa, vel_z, vel_y), depths):
        for source, target in ((planes - deep, to_next), (0, to_prev)):
            copies.append(
                pltpu.make_async_copy(
                    field.at[pl.ds(source, deep)],
                    target.at[pl.ds(at, deep)],
                    arrived.at[len(copies)],
                )
            )
        at += deep
    for copy in copies:
        copy.start()
    for copy in copies:
        copy.wait()


def deep_planes(fields, low, high):
    planes = fields[0].shape[0]
    at = 0
    columns = []
    for field, deep in zip(fields, depths):
        column = [(low, at + i, 1 + i) for i in range(deep)]
        column += [(field, i, 1 + deep) for i in range(planes)]
        column += [(high, at + i, deep - i) for i in range(deep)]
        columns.append(column)
        at += deep
    return columns


def rows_kernel(fuel, heat, kappa, vel_z, vel_y, low, high, to_next, to_prev):
    rows = fuel.shape[1]
    at = 0
    for column in deep_planes((fuel, heat, kappa, vel_z, vel_y), low, high):
        for source, i, width in column:
            to_next[at : at + width] = source[i, rows - width : rows]
            to_prev[at : at + width] = source[i, 0:width]
            at += width


def side(value, step):
    size = value.shape[1]
    lane = lax.broadcasted_iota(jnp.int32, value.shape, 1)
    if step > 0:
        return jnp.where(lane < size - 1, pltpu.roll(value, size - 1, 1), 0.0)
    return jnp.where(lane > 0, pltpu.roll(value, 1, 1), 0.0)


def above(value):
    return pltpu.roll(value, value.shape[0] - 1, 0)


def below(value):
    return pltpu.roll(value, 1, 0)


def parts(ref, i, vel_z, vel_y):
    centre = ref[i]
    ahead, behind = ref[i + 1], ref[i - 1]
    up, down = above(centre), below(centre)
    near = (ahead + behind) + (up + down) + (side(centre, 1) + side(centre, -1))
    transport = 0.5 * (vel_z * (ahead - behind) + vel_y * (up - down))
    return centre, near - 6.0 * centre, transport


def rates(fuel_ref, heat_ref, i, kappa, vel_z, vel_y):
    fuel_mid, fuel_lap, fuel_adv = parts(fuel_ref, i, vel_z, vel_y)
    heat_mid, heat_lap, heat_adv = parts(heat_ref, i, vel_z, vel_y)
    square = heat_mid * heat_mid
    burning = burn_rate * fuel_mid * square / (1.0 + square)
    return (
        lewis_ratio * kappa * fuel_lap - fuel_adv - burning,
        kappa * heat_lap - heat_adv + heat_release * burning,
    )


def block_transpose(tile):
    row = lax.broadcasted_iota(jnp.int32, tile.shape, 0)
    block = lax.broadcasted_iota(jnp.int32, tile.shape, 1) // 16
    for bit in (1, 2, 4):
        later = pltpu.roll(pltpu.roll(tile, 8 - bit, 0), 16 * bit, 1)
        earlier = pltpu.roll(pltpu.roll(tile, bit, 0), 128 - 16 * bit, 1)
        row_bit, block_bit = (row & bit) != 0, (block & bit) != 0
        swapped = jnp.where(block_bit, later, earlier)
        tile = jnp.where(row_bit == block_bit, tile, swapped)
    return tile


def step_kernel(
    fuel, heat, kappa, vel_z, vel_y, low, high, row_low, row_high, out,
    fuel_s, heat_s, kappa_s, vel_z_s, vel_y_s, fuel_one, heat_one, heat_two, fuel_two, edge,
):
    planes, rows, size = fuel.shape
    tall = fuel_s.shape[1]
    own = slice(0, rows)
    at = 0
    whole = (fuel_s, heat_s, kappa_s, vel_z_s, vel_y_s)
    columns = deep_planes((fuel, heat, kappa, vel_z, vel_y), low, high)
    for target, column in zip(whole, columns):
        for j, (source, i, width) in enumerate(column):
            target[j, own] = source[i]
            target[j, tall - width : tall] = row_low[at : at + width]
            target[j, rows : rows + width] = row_high[at : at + width]
            at += width

    def first(j, carry):
        rate_fuel, rate_heat = rates(
            fuel_s, heat_s, j + 1, kappa_s[j], vel_z_s[j], vel_y_s[j]
        )
        fuel_one[j] = fuel_s[j + 1] + time_step * rate_fuel
        heat_one[j] = heat_s[j + 1] + time_step * rate_heat
        return carry

    lax.fori_loop(0, planes + 2, first, 0)

    def second(j, carry):
        rate_fuel, rate_heat = rates(
            fuel_one, heat_one, j + 1, kappa_s[j + 1], vel_z_s[j + 1], vel_y_s[j + 1]
        )
        fuel_two[j] = 0.5 * (fuel_s[j + 2] + fuel_one[j + 1] + time_step * rate_fuel)
        heat_two[j] = 0.5 * (heat_s[j + 2] + heat_one[j + 1] + time_step * rate_heat)
        return carry

    lax.fori_loop(0, planes, second, 0)

    chunk = 2 * planes + 2
    count = size // 16

    def send(value, at):
        for m in range(size // 128):
            tile = block_transpose(value[:, m * 128 : (m + 1) * 128])
            place = (8 * m - first_member(count)) % count
            before = min(8, count - place)
            out[pl.ds(place * chunk + at, before, stride=chunk), :] = tile[:before]
            if before < 8:
                out[pl.ds(at, 8 - before, stride=chunk), :] = tile[before:]

    lane = lax.broadcasted_iota(jnp.int32, (rows, size), 1)
    place = lane % 16
    borders = jnp.zeros((rows, size), jnp.float32)
    for p in range(planes):
        level = heat_two[p, own]
        send(level, p)
        send(fuel_two[p, own], planes + p)
        edge[p : p + 1] = heat_two[p, tall - 1 : tall]
        edge[planes + p : planes + p + 1] = heat_two[p, rows : rows + 1]
        left = (place == p) & (lane >= 16)
        right = (place == planes + p) & (lane < size - 16)
        borders = jnp.where(left, pltpu.roll(level, p + 1, 1), borders)
        borders = jnp.where(right, pltpu.roll(level, size - 16 + planes + p, 1), borders)
    send(edge[...], 2 * planes)
    send(borders, 2 * planes + 1)


def per_function(ref, *index):
    row = lax.broadcasted_iota(jnp.int32, (8, 128), 0)
    value = jnp.full((8, 128), ref[(0,) + index], jnp.float32)
    for k in range(1, 8):
        value = jnp.where(row == k, ref[(k,) + index], value)
    return value


def shift_rows(value, step):
    size = value.shape[0]
    row = lax.broadcasted_iota(jnp.int32, value.shape, 0)
    start = (size - first_member(size)) % size
    if step > 0:
        return jnp.where(row != (start - 1) % size, pltpu.roll(value, size - 1, 0), 0.0)
    return jnp.where(row != start, pltpu.roll(value, 1, 0), 0.0)


def march_kernel(opacity_scale, planes, centre, width, density, tint, fields, out, lights):
    chunk = 2 * planes + 2
    count = fields.shape[0] // chunk
    columns = [fields[pl.ds(i, count, stride=chunk), :] for i in range(planes)]
    edge, borders = (
        fields[pl.ds(2 * planes + i, count, stride=chunk), :] for i in range(2)
    )
    lane = lax.broadcasted_iota(jnp.int32, (count, 128), 1)
    place = lane % 16
    for p in range(planes):
        level = columns[p]
        ahead = columns[p + 1] if p + 1 < planes else shift_rows(columns[0], 1)
        behind = columns[p - 1] if p > 0 else shift_rows(columns[planes - 1], -1)

        def moved(value, by):
            by = by % 128
            return pltpu.roll(value, by, 1) if by else value

        up = jnp.where(lane < 112, moved(level, -16), moved(edge, 112 - 16 * (planes + p)))
        down = jnp.where(lane >= 16, moved(level, 16), moved(edge, -16 * p))
        right = jnp.where(place < 15, moved(level, -1), moved(borders, 15 - planes - p))
        left = jnp.where(place > 0, moved(level, 1), moved(borders, -p))
        grad_z, grad_y, grad_x = 0.5 * (ahead - behind), 0.5 * (up - down), 0.5 * (right - left)
        norm_sq = grad_z * grad_z + grad_y * grad_y + grad_x * grad_x + 1.0
        facing = 0.48 * grad_z + 0.6 * grad_y + 0.64 * grad_x
        lights[p] = 0.5 * (0.35 + 0.65 * (facing * facing) / norm_sq)

    mid = per_function(centre)
    spread = per_function(width)
    narrow = -log2_e / (spread * spread)
    thick = per_function(density) * (-log2_e * opacity_scale)
    half = [0.5 * per_function(tint, c) for c in range(3)]

    def one_plane(s, p, state):
        passing, total, *colour = state
        s = lax.rem(s + (count - first_member(count)), count)
        at = s * chunk + p
        level, fuel = fields[pl.ds(at, 1), :], fields[pl.ds(at + planes, 1), :]
        offset = level - mid
        survive = jnp.exp2(thick * jnp.exp2(narrow * (offset * offset)))
        weight = passing * (1.0 - survive) * lights[p, pl.ds(s, 1)]
        colour = [value + weight * jnp.tanh(half[c] * fuel) for c, value in enumerate(colour)]
        return (passing * survive, total + weight, *colour)

    joint = 4

    def segments(i, state):
        for s in range(joint):
            for p in range(planes):
                state = one_plane(i * joint + s, p, state)
        return state

    zero = jnp.zeros((8, 128), jnp.float32)
    state = lax.fori_loop(0, count // joint, segments, (zero + 1.0, zero, zero, zero, zero))
    passing, total, *colour = state
    for c, value in enumerate([total + value for value in colour] + [passing]):
        tile = block_transpose(value)
        for k in range(8):
            out[k, c] = tile[:, 16 * k : 16 * k + 16]


def body(fuel, heat, kappa, vel_z, vel_y, tf_centre, tf_width, tf_density, tf_tint):
    planes, rows, columns = fuel.shape
    depth_count = lax.axis_size("depth")
    fields = (fuel, heat, kappa, vel_z, vel_y)
    f32 = functools.partial(jax.ShapeDtypeStruct, dtype=jnp.float32)
    sent_planes = sum(depths)
    sent_rows = sum(planes * (1 + deep) + deep * (1 + deep) for deep in depths)

    to_next, to_prev = pl.pallas_call(
        planes_kernel,
        out_shape=[f32((sent_planes, rows, columns))] * 2,
        in_specs=[hbm] * 5,
        out_specs=[vmem] * 2,
        scratch_shapes=[pltpu.SemaphoreType.DMA((2 * len(depths),))],
        compiler_params=params(),
        name="pack_planes",
    )(*(pltpu.with_memory_space_constraint(field, pltpu.HBM) for field in fields))
    low, high = exchange(to_next, to_prev, "depth")
    to_next, to_prev = pl.pallas_call(
        rows_kernel,
        out_shape=[f32((sent_rows, columns))] * 2,
        in_specs=[vmem] * 7,
        out_specs=[vmem] * 2,
        compiler_params=params(),
        name="pack_rows",
    )(*fields, low, high)
    row_low, row_high = exchange(to_next, to_prev, "rows")

    tall = rows + 8
    chunk = 2 * planes + 2
    scratch = [pltpu.VMEM((planes + 2 * deep, tall, columns), jnp.float32) for deep in depths]
    scratch += [pltpu.VMEM((planes + 2, tall, columns), jnp.float32)] * 2
    scratch += [pltpu.VMEM((planes, tall, columns), jnp.float32)] * 2
    scratch += [pltpu.VMEM((2 * planes, columns), jnp.float32)]
    stepped = pl.pallas_call(
        step_kernel,
        out_shape=f32((depth_count * chunk, 128)),
        in_specs=[vmem] * 9,
        out_specs=vmem,
        scratch_shapes=scratch,
        compiler_params=params(),
        name="step",
    )(*fields, low, high, row_low, row_high)

    order = [(first_member(depth_count) + i) % depth_count for i in range(depth_count)]
    gathered = lax.all_to_all(
        stepped.reshape(depth_count, 1, chunk * 128),
        "depth",
        split_axis=0,
        concat_axis=0,
        axis_index_groups=[order],
        tiled=True,
    ).reshape(depth_count * chunk, 128)

    return pl.pallas_call(
        functools.partial(march_kernel, 4.0 / (planes * depth_count), planes),
        out_shape=f32((8, 4, rows, columns // depth_count)),
        in_specs=[smem] * 4 + [vmem],
        out_specs=vmem,
        scratch_shapes=[pltpu.VMEM((planes, depth_count, 128), jnp.float32)],
        compiler_params=params(),
        name="march",
    )(tf_centre, tf_width, tf_density, tf_tint, gathered)


def solution(mesh):
    placed = (P("depth", "rows", None),) * 5 + (P(),) * 4
    return jax.shard_map(
        body, mesh=mesh, in_specs=placed, out_specs=P(None, None, "rows", "depth"), check_vma=False
    )
```

```python
import functools
import math

import jax
import jax.numpy as jnp
from jax import lax
from jax.experimental import pallas as pl
from jax.experimental.pallas import tpu as pltpu
from jax.sharding import PartitionSpec as P

time_step = 1.0
lewis_ratio = 0.8
heat_release = 0.6
burn_rate = 0.5

depths = (2, 2, 1, 1, 1)
log2_e = math.log2(math.e)

vmem = pl.BlockSpec(memory_space=pltpu.VMEM)
smem = pl.BlockSpec(memory_space=pltpu.SMEM)
hbm = pl.BlockSpec(memory_space=pltpu.HBM)


def first_member(count):
    return 5 * count // 8


def exchange(to_next, to_prev, axis):
    count = lax.axis_size(axis)
    forward = [(i, i + 1) for i in range(count - 1)]
    backward = [(target, source) for source, target in forward]
    return lax.ppermute(to_next, axis, forward), lax.ppermute(to_prev, axis, backward)


def swap(block, axis, first):
    count = lax.axis_size(axis)
    forward = [(i, i + 1) for i in range(first, count - 1, 2)]
    return lax.ppermute(block, axis, forward + [(target, source) for source, target in forward])


def second_core():
    return lax.rem(lax.axis_index("rows"), 2) == 1


def params(**more):
    return pltpu.CompilerParams(vmem_limit_bytes=8 << 20, **more)


def planes_kernel(fuel, heat, kappa, vel_z, vel_y, to_next, to_prev, arrived):
    planes = fuel.shape[0]
    at, copies = 0, []
    for field, deep in zip((fuel, heat, kappa, vel_z, vel_y), depths):
        for source, target in ((planes - deep, to_next), (0, to_prev)):
            copies.append(
                pltpu.make_async_copy(
                    field.at[pl.ds(source, deep)],
                    target.at[pl.ds(at, deep)],
                    arrived.at[len(copies)],
                )
            )
        at += deep
    for copy in copies:
        copy.start()
    for copy in copies:
        copy.wait()


def deep_planes(fields, low, high):
    planes = fields[0].shape[0]
    at = 0
    columns = []
    for field, deep in zip(fields, depths):
        column = [(low, at + i, 1 + i) for i in range(deep)]
        column += [(field, i, 1 + deep) for i in range(planes)]
        column += [(high, at + i, deep - i) for i in range(deep)]
        columns.append(column)
        at += deep
    return columns


def rows_kernel(fuel, heat, kappa, vel_z, vel_y, low, high, outer, inner):
    rows = fuel.shape[1]
    columns = deep_planes((fuel, heat, kappa, vel_z, vel_y), low, high)

    def fill(to_next, to_prev):
        at = 0
        for column in columns:
            for source, i, width in column:
                to_next[at : at + width] = source[i, rows - width : rows]
                to_prev[at : at + width] = source[i, 0:width]
                at += width

    odd = second_core()
    pl.when(odd)(lambda: fill(outer, inner))
    pl.when(jnp.logical_not(odd))(lambda: fill(inner, outer))


def side(value, step):
    size = value.shape[1]
    lane = lax.broadcasted_iota(jnp.int32, value.shape, 1)
    if step > 0:
        return jnp.where(lane < size - 1, pltpu.roll(value, size - 1, 1), 0.0)
    return jnp.where(lane > 0, pltpu.roll(value, 1, 1), 0.0)


def above(value):
    return pltpu.roll(value, value.shape[0] - 1, 0)


def below(value):
    return pltpu.roll(value, 1, 0)


def parts(ref, i, vel_z, vel_y):
    centre = ref[i]
    ahead, behind = ref[i + 1], ref[i - 1]
    up, down = above(centre), below(centre)
    near = (ahead + behind) + (up + down) + (side(centre, 1) + side(centre, -1))
    transport = 0.5 * (vel_z * (ahead - behind) + vel_y * (up - down))
    return centre, near - 6.0 * centre, transport


def rates(fuel_ref, heat_ref, i, kappa, vel_z, vel_y):
    fuel_mid, fuel_lap, fuel_adv = parts(fuel_ref, i, vel_z, vel_y)
    heat_mid, heat_lap, heat_adv = parts(heat_ref, i, vel_z, vel_y)
    square = heat_mid * heat_mid
    burning = burn_rate * fuel_mid * square / (1.0 + square)
    return (
        lewis_ratio * kappa * fuel_lap - fuel_adv - burning,
        kappa * heat_lap - heat_adv + heat_release * burning,
    )


def block_transpose(tile):
    row = lax.broadcasted_iota(jnp.int32, tile.shape, 0)
    block = lax.broadcasted_iota(jnp.int32, tile.shape, 1) // 16
    for bit in (1, 2, 4):
        later = pltpu.roll(pltpu.roll(tile, 8 - bit, 0), 16 * bit, 1)
        earlier = pltpu.roll(pltpu.roll(tile, bit, 0), 128 - 16 * bit, 1)
        row_bit, block_bit = (row & bit) != 0, (block & bit) != 0
        swapped = jnp.where(block_bit, later, earlier)
        tile = jnp.where(row_bit == block_bit, tile, swapped)
    return tile


def step_kernel(
    fuel, heat, kappa, vel_z, vel_y, low, high, outer, inner, out,
    fuel_s, heat_s, kappa_s, vel_z_s, vel_y_s, fuel_one, heat_one, heat_two, fuel_two, edge,
):
    planes, rows, size = fuel.shape
    tall = fuel_s.shape[1]
    own = slice(0, rows)
    whole = (fuel_s, heat_s, kappa_s, vel_z_s, vel_y_s)
    columns = deep_planes((fuel, heat, kappa, vel_z, vel_y), low, high)
    for target, column in zip(whole, columns):
        for j, (source, i, width) in enumerate(column):
            target[j, own] = source[i]

    def border(row_low, row_high):
        at = 0
        for target, column in zip(whole, columns):
            for j, (source, i, width) in enumerate(column):
                target[j, tall - width : tall] = row_low[at : at + width]
                target[j, rows : rows + width] = row_high[at : at + width]
                at += width

    odd = second_core()
    pl.when(odd)(lambda: border(inner, outer))
    pl.when(jnp.logical_not(odd))(lambda: border(outer, inner))

    def first(j, carry):
        rate_fuel, rate_heat = rates(
            fuel_s, heat_s, j + 1, kappa_s[j], vel_z_s[j], vel_y_s[j]
        )
        fuel_one[j] = fuel_s[j + 1] + time_step * rate_fuel
        heat_one[j] = heat_s[j + 1] + time_step * rate_heat
        return carry

    lax.fori_loop(0, planes + 2, first, 0)

    def second(j, carry):
        rate_fuel, rate_heat = rates(
            fuel_one, heat_one, j + 1, kappa_s[j + 1], vel_z_s[j + 1], vel_y_s[j + 1]
        )
        fuel_two[j] = 0.5 * (fuel_s[j + 2] + fuel_one[j + 1] + time_step * rate_fuel)
        heat_two[j] = 0.5 * (heat_s[j + 2] + heat_one[j + 1] + time_step * rate_heat)
        return carry

    lax.fori_loop(0, planes, second, 0)

    chunk = 2 * planes + 2
    count = size // 16

    def send(value, at):
        for m in range(size // 128):
            tile = block_transpose(value[:, m * 128 : (m + 1) * 128])
            place = (8 * m - first_member(count)) % count
            before = min(8, count - place)
            out[pl.ds(place * chunk + at, before, stride=chunk), :] = tile[:before]
            if before < 8:
                out[pl.ds(at, 8 - before, stride=chunk), :] = tile[before:]

    lane = lax.broadcasted_iota(jnp.int32, (rows, size), 1)
    place = lane % 16
    borders = jnp.zeros((rows, size), jnp.float32)
    for p in range(planes):
        level = heat_two[p, own]
        send(level, p)
        send(fuel_two[p, own], planes + p)
        edge[p : p + 1] = heat_two[p, tall - 1 : tall]
        edge[planes + p : planes + p + 1] = heat_two[p, rows : rows + 1]
        left = (place == p) & (lane >= 16)
        right = (place == planes + p) & (lane < size - 16)
        borders = jnp.where(left, pltpu.roll(level, p + 1, 1), borders)
        borders = jnp.where(right, pltpu.roll(level, size - 16 + planes + p, 1), borders)
    send(edge[...], 2 * planes)
    send(borders, 2 * planes + 1)


def per_function(ref, *index):
    row = lax.broadcasted_iota(jnp.int32, (8, 128), 0)
    value = jnp.full((8, 128), ref[(0,) + index], jnp.float32)
    for k in range(1, 8):
        value = jnp.where(row == k, ref[(k,) + index], value)
    return value


def shift_rows(value, step):
    size = value.shape[0]
    row = lax.broadcasted_iota(jnp.int32, value.shape, 0)
    start = (size - first_member(size)) % size
    if step > 0:
        return jnp.where(row != (start - 1) % size, pltpu.roll(value, size - 1, 0), 0.0)
    return jnp.where(row != start, pltpu.roll(value, 1, 0), 0.0)


def march_kernel(opacity_scale, planes, centre, width, density, tint, fields, out, lights):
    chunk = 2 * planes + 2
    count = fields.shape[0] // chunk
    columns = [fields[pl.ds(i, count, stride=chunk), :] for i in range(planes)]
    edge, borders = (
        fields[pl.ds(2 * planes + i, count, stride=chunk), :] for i in range(2)
    )
    lane = lax.broadcasted_iota(jnp.int32, (count, 128), 1)
    place = lane % 16
    for p in range(planes):
        level = columns[p]
        ahead = columns[p + 1] if p + 1 < planes else shift_rows(columns[0], 1)
        behind = columns[p - 1] if p > 0 else shift_rows(columns[planes - 1], -1)

        def moved(value, by):
            by = by % 128
            return pltpu.roll(value, by, 1) if by else value

        up = jnp.where(lane < 112, moved(level, -16), moved(edge, 112 - 16 * (planes + p)))
        down = jnp.where(lane >= 16, moved(level, 16), moved(edge, -16 * p))
        right = jnp.where(place < 15, moved(level, -1), moved(borders, 15 - planes - p))
        left = jnp.where(place > 0, moved(level, 1), moved(borders, -p))
        grad_z, grad_y, grad_x = 0.5 * (ahead - behind), 0.5 * (up - down), 0.5 * (right - left)
        norm_sq = grad_z * grad_z + grad_y * grad_y + grad_x * grad_x + 1.0
        facing = 0.48 * grad_z + 0.6 * grad_y + 0.64 * grad_x
        lights[p] = 0.5 * (0.35 + 0.65 * (facing * facing) / norm_sq)

    mid = per_function(centre)
    spread = per_function(width)
    narrow = -log2_e / (spread * spread)
    thick = per_function(density) * (-log2_e * opacity_scale)
    half = [0.5 * per_function(tint, c) for c in range(3)]

    def one_plane(s, p, state):
        passing, total, *colour = state
        s = lax.rem(s + (count - first_member(count)), count)
        at = s * chunk + p
        level, fuel = fields[pl.ds(at, 1), :], fields[pl.ds(at + planes, 1), :]
        offset = level - mid
        survive = jnp.exp2(thick * jnp.exp2(narrow * (offset * offset)))
        weight = passing * (1.0 - survive) * lights[p, pl.ds(s, 1)]
        colour = [value + weight * jnp.tanh(half[c] * fuel) for c, value in enumerate(colour)]
        return (passing * survive, total + weight, *colour)

    joint = 4

    def segments(i, state):
        for s in range(joint):
            for p in range(planes):
                state = one_plane(i * joint + s, p, state)
        return state

    zero = jnp.zeros((8, 128), jnp.float32)
    state = lax.fori_loop(0, count // joint, segments, (zero + 1.0, zero, zero, zero, zero))
    passing, total, *colour = state
    for c, value in enumerate([total + value for value in colour] + [passing]):
        tile = block_transpose(value)
        for k in range(8):
            out[k, c] = tile[:, 16 * k : 16 * k + 16]


def body(fuel, heat, kappa, vel_z, vel_y, tf_centre, tf_width, tf_density, tf_tint):
    planes, rows, columns = fuel.shape
    depth_count = lax.axis_size("depth")
    fields = (fuel, heat, kappa, vel_z, vel_y)
    f32 = functools.partial(jax.ShapeDtypeStruct, dtype=jnp.float32)
    sent_planes = sum(depths)
    sent_rows = sum(planes * (1 + deep) + deep * (1 + deep) for deep in depths)

    to_next, to_prev = pl.pallas_call(
        planes_kernel,
        out_shape=[f32((sent_planes, rows, columns))] * 2,
        in_specs=[hbm] * 5,
        out_specs=[vmem] * 2,
        scratch_shapes=[pltpu.SemaphoreType.DMA((2 * len(depths),))],
        compiler_params=params(),
        name="pack_planes",
    )(*(pltpu.with_memory_space_constraint(field, pltpu.HBM) for field in fields))
    low, high = exchange(to_next, to_prev, "depth")
    outer, inner = pl.pallas_call(
        rows_kernel,
        out_shape=[f32((sent_rows, columns))] * 2,
        in_specs=[vmem] * 7,
        out_specs=[vmem] * 2,
        compiler_params=params(),
        name="pack_rows",
    )(*fields, low, high)
    outer, inner = swap(outer, "rows", 1), swap(inner, "rows", 0)

    tall = rows + 8
    chunk = 2 * planes + 2
    scratch = [pltpu.VMEM((planes + 2 * deep, tall, columns), jnp.float32) for deep in depths]
    scratch += [pltpu.VMEM((planes + 2, tall, columns), jnp.float32)] * 2
    scratch += [pltpu.VMEM((planes, tall, columns), jnp.float32)] * 2
    scratch += [pltpu.VMEM((2 * planes, columns), jnp.float32)]
    stepped = pl.pallas_call(
        step_kernel,
        out_shape=f32((depth_count * chunk, 128)),
        in_specs=[vmem] * 9,
        out_specs=vmem,
        scratch_shapes=scratch,
        compiler_params=params(),
        name="step",
    )(*fields, low, high, outer, inner)

    order = [(first_member(depth_count) + i) % depth_count for i in range(depth_count)]
    gathered = lax.all_to_all(
        stepped.reshape(depth_count, 1, chunk * 128),
        "depth",
        split_axis=0,
        concat_axis=0,
        axis_index_groups=[order],
        tiled=True,
    ).reshape(depth_count * chunk, 128)

    return pl.pallas_call(
        functools.partial(march_kernel, 4.0 / (planes * depth_count), planes),
        out_shape=f32((8, 4, rows, columns // depth_count)),
        in_specs=[smem] * 4 + [vmem],
        out_specs=vmem,
        scratch_shapes=[pltpu.VMEM((planes, depth_count, 128), jnp.float32)],
        compiler_params=params(),
        name="march",
    )(tf_centre, tf_width, tf_density, tf_tint, gathered)


def solution(mesh):
    placed = (P("depth", "rows", None),) * 5 + (P(),) * 4
    return jax.shard_map(
        body, mesh=mesh, in_specs=placed, out_specs=P(None, None, "rows", "depth"), check_vma=False
    )
```

```python
import functools
import math

import jax
import jax.numpy as jnp
from jax import lax
from jax.experimental import pallas as pl
from jax.experimental.pallas import tpu as pltpu
from jax.sharding import PartitionSpec as P

time_step = 1.0
lewis_ratio = 0.8
heat_release = 0.6
burn_rate = 0.5

depths = (2, 2, 1, 1, 1)
log2_e = math.log2(math.e)

vmem = pl.BlockSpec(memory_space=pltpu.VMEM)
smem = pl.BlockSpec(memory_space=pltpu.SMEM)
hbm = pl.BlockSpec(memory_space=pltpu.HBM)


def first_member(count):
    return 5 * count // 8


def exchange(to_next, to_prev, axis):
    count = lax.axis_size(axis)
    forward = [(i, i + 1) for i in range(count - 1)]
    backward = [(target, source) for source, target in forward]
    return lax.ppermute(to_next, axis, forward), lax.ppermute(to_prev, axis, backward)


def swap(block, axis, first):
    count = lax.axis_size(axis)
    forward = [(i, i + 1) for i in range(first, count - 1, 2)]
    return lax.ppermute(block, axis, forward + [(target, source) for source, target in forward])


def second_core():
    return lax.rem(lax.axis_index("rows"), 2) == 1


def params(**more):
    return pltpu.CompilerParams(vmem_limit_bytes=8 << 20, **more)


def planes_kernel(fuel, heat, kappa, vel_z, vel_y, to_next, to_prev, arrived):
    planes = fuel.shape[0]
    at, copies = 0, []
    for field, deep in zip((fuel, heat, kappa, vel_z, vel_y), depths):
        for source, target in ((planes - deep, to_next), (0, to_prev)):
            copies.append(
                pltpu.make_async_copy(
                    field.at[pl.ds(source, deep)],
                    target.at[pl.ds(at, deep)],
                    arrived.at[len(copies)],
                )
            )
        at += deep
    for copy in copies:
        copy.start()
    for copy in copies:
        copy.wait()


def deep_planes(fields, low, high):
    planes = fields[0].shape[0]
    at = 0
    columns = []
    for field, deep in zip(fields, depths):
        column = [(low, at + i, 1 + i) for i in range(deep)]
        column += [(field, i, 1 + deep) for i in range(planes)]
        column += [(high, at + i, deep - i) for i in range(deep)]
        columns.append(column)
        at += deep
    return columns


def rows_kernel(fuel, heat, kappa, vel_z, vel_y, low, high, outer, inner):
    rows = fuel.shape[1]
    columns = deep_planes((fuel, heat, kappa, vel_z, vel_y), low, high)

    def fill(to_next, to_prev):
        at = 0
        for column in columns:
            for source, i, width in column:
                to_next[at : at + width] = source[i, rows - width : rows]
                to_prev[at : at + width] = source[i, 0:width]
                at += width

    odd = second_core()
    pl.when(odd)(lambda: fill(outer, inner))
    pl.when(jnp.logical_not(odd))(lambda: fill(inner, outer))


def neighbours(blocks, m, lane, rolled):
    def turned(i, by):
        if not 0 <= i < len(blocks):
            return 0.0
        if (i, by) not in rolled:
            rolled[i, by] = pltpu.roll(blocks[i], by, 1)
        return rolled[i, by]

    right = jnp.where(lane < 127, turned(m, 127), turned(m + 1, 127))
    return right + jnp.where(lane > 0, turned(m, 1), turned(m - 1, 1))


def parts(centre, ahead, behind, beside, half_z, half_y):
    up, down = pltpu.roll(centre, centre.shape[0] - 1, 0), pltpu.roll(centre, 1, 0)
    near = (ahead + behind) + (up + down) + beside
    return near - 6.0 * centre, half_z * (ahead - behind) + half_y * (up - down)


def rates(fuels, heats, kappa, vel_z, vel_y):
    half_z, half_y = 0.5 * vel_z, 0.5 * vel_y
    fuel_lap, fuel_adv = parts(*fuels, half_z, half_y)
    heat_lap, heat_adv = parts(*heats, half_z, half_y)
    square = heats[0] * heats[0]
    burning = burn_rate * fuels[0] * square / (1.0 + square)
    return (
        lewis_ratio * kappa * fuel_lap - fuel_adv - burning,
        kappa * heat_lap - heat_adv + heat_release * burning,
    )


def block_transpose(tiles):
    shape = (8, 128)
    row = lax.broadcasted_iota(jnp.int32, shape, 0)
    block = lax.broadcasted_iota(jnp.int32, shape, 1) // 16
    for bit in (4, 2, 1):
        row_bit, block_bit = (row & bit) != 0, (block & bit) != 0
        if bit == 4:
            moved = [pltpu.roll(pltpu.roll(tile, 64, 1), 4, 0) for tile in tiles]
        else:
            right = [pltpu.roll(tile, 16 * bit, 1) for tile in tiles]
            left = [pltpu.roll(tile, 128 - 16 * bit, 1) for tile in tiles]
            right = [pltpu.roll(tile, 8 - bit, 0) for tile in right]
            left = [pltpu.roll(tile, bit, 0) for tile in left]
            moved = [jnp.where(block_bit, r, l) for r, l in zip(right, left)]
        same = row_bit == block_bit
        tiles = [jnp.where(same, tile, other) for tile, other in zip(tiles, moved)]
    return tiles


def step_kernel(
    fuel, heat, kappa, vel_z, vel_y, low, high, outer, inner, out,
    halo, fuel_one, heat_one, heat_two, fuel_two, edge,
):
    planes, rows, size = fuel.shape
    columns = deep_planes((fuel, heat, kappa, vel_z, vel_y), low, high)

    def border(row_low, row_high):
        at = 0
        for j, (source, i, width) in enumerate(sum(columns, [])):
            halo[j, rows - width : rows] = row_low[at : at + width]
            halo[j, 0:width] = row_high[at : at + width]
            at += width

    odd = second_core()
    pl.when(odd)(lambda: border(inner, outer))
    pl.when(jnp.logical_not(odd))(lambda: border(outer, inner))

    parts_of = [slice(at, at + 128) for at in range(0, size, 128)]
    lane = lax.broadcasted_iota(jnp.int32, (2 * rows, 128), 1)

    def plane(field, j, m):
        source, i, width = columns[field][j]
        row = sum(len(column) for column in columns[:field]) + j
        return jnp.concatenate([source[i, :, parts_of[m]], halo[row, :, parts_of[m]]], axis=0)

    for j in range(planes + 2):
        blocks = [[plane(f, j + 1, m) for m in range(len(parts_of))] for f in (0, 1)]
        rolled = ({}, {})
        for m, part in enumerate(parts_of):
            fuels, heats = (
                (
                    blocks[f][m],
                    plane(f, j + 2, m),
                    plane(f, j, m),
                    neighbours(blocks[f], m, lane, rolled[f]),
                )
                for f in (0, 1)
            )
            rate_fuel, rate_heat = rates(fuels, heats, *(plane(f, j, m) for f in (2, 3, 4)))
            fuel_one[j, :, part] = fuels[0] + time_step * rate_fuel
            heat_one[j, :, part] = heats[0] + time_step * rate_heat

    for j in range(planes):
        ones = (fuel_one, heat_one)
        blocks = [[ref[j + 1, :, part] for part in parts_of] for ref in ones]
        rolled = ({}, {})
        for m, part in enumerate(parts_of):
            fuels, heats = (
                (
                    blocks[f][m],
                    ones[f][j + 2, :, part],
                    ones[f][j, :, part],
                    neighbours(blocks[f], m, lane, rolled[f]),
                )
                for f in (0, 1)
            )
            rate_fuel, rate_heat = rates(fuels, heats, *(plane(f, j + 1, m) for f in (2, 3, 4)))
            final = 0.5 * (plane(0, j + 2, m) + fuels[0] + time_step * rate_fuel)
            fuel_two[j, :, part] = final[:rows]
            heat_two[j, :, part] = 0.5 * (plane(1, j + 2, m) + heats[0] + time_step * rate_heat)

    chunk = 2 * planes + 2
    count = size // 16

    def send(values, at):
        groups = size // 128
        tiles = [value[:, m * 128 : (m + 1) * 128] for value in values for m in range(groups)]
        for i, tile in enumerate(block_transpose(tiles)):
            row, m = at + i // groups, i % groups
            place = (8 * m - first_member(count)) % count
            before = min(8, count - place)
            out[pl.ds(place * chunk + row, before, stride=chunk), :] = tile[:before]
            if before < 8:
                out[pl.ds(row, 8 - before, stride=chunk), :] = tile[before:]

    lane = lax.broadcasted_iota(jnp.int32, (rows, size), 1)
    place = lane % 16
    borders = jnp.zeros((rows, size), jnp.float32)
    for p in range(planes):
        level = heat_two[p, :rows]
        send([level], p)
        send([fuel_two[p]], planes + p)
        edge[p : p + 1] = heat_two[p, 2 * rows - 1 : 2 * rows]
        edge[planes + p : planes + p + 1] = heat_two[p, rows : rows + 1]
        left = (place == p) & (lane >= 16)
        right = (place == planes + p) & (lane < size - 16)
        borders = jnp.where(left, pltpu.roll(level, p + 1, 1), borders)
        borders = jnp.where(right, pltpu.roll(level, size - 16 + planes + p, 1), borders)
    send([edge[...]], 2 * planes)
    send([borders], 2 * planes + 1)


def per_function(ref, *index):
    row = lax.broadcasted_iota(jnp.int32, (8, 128), 0)
    value = jnp.full((8, 128), ref[(0,) + index], jnp.float32)
    for k in range(1, 8):
        value = jnp.where(row == k, ref[(k,) + index], value)
    return value


def shift_rows(value, step):
    size = value.shape[0]
    row = lax.broadcasted_iota(jnp.int32, value.shape, 0)
    start = (size - first_member(size)) % size
    if step > 0:
        return jnp.where(row != (start - 1) % size, pltpu.roll(value, size - 1, 0), 0.0)
    return jnp.where(row != start, pltpu.roll(value, 1, 0), 0.0)


def march_kernel(opacity_scale, planes, centre, width, density, tint, fields, out, lights):
    chunk = 2 * planes + 2
    count = fields.shape[0] // chunk
    columns = [fields[pl.ds(i, count, stride=chunk), :] for i in range(planes)]
    edge, borders = (
        fields[pl.ds(2 * planes + i, count, stride=chunk), :] for i in range(2)
    )
    lane = lax.broadcasted_iota(jnp.int32, (count, 128), 1)
    place = lane % 16
    for p in range(planes):
        level = columns[p]
        ahead = columns[p + 1] if p + 1 < planes else shift_rows(columns[0], 1)
        behind = columns[p - 1] if p > 0 else shift_rows(columns[planes - 1], -1)

        def moved(value, by):
            by = by % 128
            return pltpu.roll(value, by, 1) if by else value

        up = jnp.where(lane < 112, moved(level, -16), moved(edge, 112 - 16 * (planes + p)))
        down = jnp.where(lane >= 16, moved(level, 16), moved(edge, -16 * p))
        right = jnp.where(place < 15, moved(level, -1), moved(borders, 15 - planes - p))
        left = jnp.where(place > 0, moved(level, 1), moved(borders, -p))
        grad_z, grad_y, grad_x = 0.5 * (ahead - behind), 0.5 * (up - down), 0.5 * (right - left)
        norm_sq = grad_z * grad_z + grad_y * grad_y + grad_x * grad_x + 1.0
        facing = 0.48 * grad_z + 0.6 * grad_y + 0.64 * grad_x
        lights[p] = 0.5 * (0.35 + 0.65 * (facing * facing) / norm_sq)

    mid = per_function(centre)
    spread = per_function(width)
    narrow = -log2_e / (spread * spread)
    thick = per_function(density) * (-log2_e * opacity_scale)
    half = [0.5 * per_function(tint, c) for c in range(3)]

    def one_plane(at, s, p, state):
        passing, total, *colour = state
        level, fuel = fields[pl.ds(at + p, 1), :], fields[pl.ds(at + planes + p, 1), :]
        offset = level - mid
        survive = jnp.exp2(thick * jnp.exp2(narrow * (offset * offset)))
        left = passing * survive
        weight = (passing - left) * lights[p, pl.ds(s, 1)]
        colour = [value + weight * jnp.tanh(half[c] * fuel) for c, value in enumerate(colour)]
        return (left, total + weight, *colour)

    joint = 8

    def segments(i, state):
        for s in range(joint):
            s = lax.rem(i * joint + s + (count - first_member(count)), count)
            for p in range(planes):
                state = one_plane(s * chunk, s, p, state)
        return state

    zero = jnp.zeros((8, 128), jnp.float32)
    state = lax.fori_loop(0, count // joint, segments, (zero + 1.0, zero, zero, zero, zero))
    passing, total, *colour = state
    values = [total + value for value in colour] + [passing]
    for c, tile in enumerate(block_transpose(values)):
        for k in range(8):
            out[k, c] = tile[:, 16 * k : 16 * k + 16]


def body(fuel, heat, kappa, vel_z, vel_y, tf_centre, tf_width, tf_density, tf_tint):
    planes, rows, columns = fuel.shape
    depth_count = lax.axis_size("depth")
    fields = (fuel, heat, kappa, vel_z, vel_y)
    f32 = functools.partial(jax.ShapeDtypeStruct, dtype=jnp.float32)
    sent_planes = sum(depths)
    sent_rows = sum(planes * (1 + deep) + deep * (1 + deep) for deep in depths)

    to_next, to_prev = pl.pallas_call(
        planes_kernel,
        out_shape=[f32((sent_planes, rows, columns))] * 2,
        in_specs=[hbm] * 5,
        out_specs=[vmem] * 2,
        scratch_shapes=[pltpu.SemaphoreType.DMA((2 * len(depths),))],
        compiler_params=params(),
        name="pack_planes",
    )(*(pltpu.with_memory_space_constraint(field, pltpu.HBM) for field in fields))
    low, high = exchange(to_next, to_prev, "depth")
    outer, inner = pl.pallas_call(
        rows_kernel,
        out_shape=[f32((sent_rows, columns))] * 2,
        in_specs=[vmem] * 7,
        out_specs=[vmem] * 2,
        compiler_params=params(),
        name="pack_rows",
    )(*fields, low, high)
    outer, inner = swap(outer, "rows", 1), swap(inner, "rows", 0)

    chunk = 2 * planes + 2
    tall = 2 * rows
    deep_count = sum(planes + 2 * deep for deep in depths)
    scratch = [pltpu.VMEM((deep_count, rows, columns), jnp.float32)]
    scratch += [pltpu.VMEM((planes + 2, tall, columns), jnp.float32)] * 2
    scratch += [pltpu.VMEM((planes, tall, columns), jnp.float32)]
    scratch += [pltpu.VMEM((planes, rows, columns), jnp.float32)]
    scratch += [pltpu.VMEM((2 * planes, columns), jnp.float32)]
    stepped = pl.pallas_call(
        step_kernel,
        out_shape=f32((depth_count * chunk, 128)),
        in_specs=[vmem] * 9,
        out_specs=vmem,
        scratch_shapes=scratch,
        compiler_params=params(),
        name="step",
    )(*fields, low, high, outer, inner)

    order = [(first_member(depth_count) + i) % depth_count for i in range(depth_count)]
    gathered = lax.all_to_all(
        stepped.reshape(depth_count, 1, chunk * 128),
        "depth",
        split_axis=0,
        concat_axis=0,
        axis_index_groups=[order],
        tiled=True,
    ).reshape(depth_count * chunk, 128)

    return pl.pallas_call(
        functools.partial(march_kernel, 4.0 / (planes * depth_count), planes),
        out_shape=f32((8, 4, rows, columns // depth_count)),
        in_specs=[smem] * 4 + [vmem],
        out_specs=vmem,
        scratch_shapes=[pltpu.VMEM((planes, depth_count, 128), jnp.float32)],
        compiler_params=params(),
        name="march",
    )(tf_centre, tf_width, tf_density, tf_tint, gathered)


def solution(mesh):
    placed = (P("depth", "rows", None),) * 5 + (P(),) * 4
    return jax.shard_map(
        body, mesh=mesh, in_specs=placed, out_specs=P(None, None, "rows", "depth"), check_vma=False
    )
```

```python
import functools
import math

import jax
import jax.numpy as jnp
from jax import lax
from jax.experimental import pallas as pl
from jax.experimental.pallas import tpu as pltpu
from jax.sharding import PartitionSpec as P

time_step = 1.0
lewis_ratio = 0.8
heat_release = 0.6
burn_rate = 0.5

befores = (3, 3, 2, 2, 2)
afters = (1, 1, 0, 0, 0)
depths = (2, 2, 1, 1, 1)
log2_e = math.log2(math.e)

vmem = pl.BlockSpec(memory_space=pltpu.VMEM)
smem = pl.BlockSpec(memory_space=pltpu.SMEM)
hbm = pl.BlockSpec(memory_space=pltpu.HBM)


def first_member(count):
    return 5 * count // 8


def exchange(to_next, to_prev, axis):
    count = lax.axis_size(axis)
    forward = [(i, (i + 1) % count) for i in range(count)]
    backward = [(i + 1, i) for i in range(count - 1)]
    return lax.ppermute(to_next, axis, forward), lax.ppermute(to_prev, axis, backward)


def swap(block, axis, first):
    count = lax.axis_size(axis)
    forward = [(i, i + 1) for i in range(first, count - 1, 2)]
    return lax.ppermute(block, axis, forward + [(target, source) for source, target in forward])


def second_core():
    return lax.rem(lax.axis_index("rows"), 2) == 1


def params(**more):
    return pltpu.CompilerParams(vmem_limit_bytes=8 << 20, **more)


def planes_kernel(fuel, heat, kappa, vel_z, vel_y, to_next, to_prev, arrived):
    planes = fuel.shape[0]
    fields = (fuel, heat, kappa, vel_z, vel_y)
    copies = []
    for target, widths, last in ((to_next, befores, True), (to_prev, afters, False)):
        at = 0
        for field, width in zip(fields, widths):
            if width:
                source = field.at[pl.ds(planes - width if last else 0, width)]
                copies.append((source, target.at[pl.ds(at, width)]))
            at += width
    copies = [
        pltpu.make_async_copy(source, target, arrived.at[i])
        for i, (source, target) in enumerate(copies)
    ]
    for copy in copies:
        copy.start()
    for copy in copies:
        copy.wait()


def deep_planes(fields, low, high):
    planes = fields[0].shape[0]
    at_low = at_high = 0
    columns = []
    for field, before, after, deep in zip(fields, befores, afters, depths):
        column = [(low, at_low + i) for i in range(before)]
        column += [(field, i) for i in range(planes)]
        column += [(high, at_high + i) for i in range(after)]
        last = len(column) - 1
        columns.append(
            [(*plane, 1 + min(deep, j, last - j)) for j, plane in enumerate(column)]
        )
        at_low, at_high = at_low + before, at_high + after
    return columns


def rows_kernel(fuel, heat, kappa, vel_z, vel_y, low, high, outer, inner):
    rows = fuel.shape[1]
    columns = deep_planes((fuel, heat, kappa, vel_z, vel_y), low, high)

    def fill(to_next, to_prev):
        at = 0
        for column in columns:
            for source, i, width in column:
                to_next[at : at + width] = source[i, rows - width : rows]
                to_prev[at : at + width] = source[i, 0:width]
                at += width

    odd = second_core()
    pl.when(odd)(lambda: fill(outer, inner))
    pl.when(jnp.logical_not(odd))(lambda: fill(inner, outer))


def neighbours(blocks, m, lane, rolled):
    def turned(i, by):
        if not 0 <= i < len(blocks):
            return 0.0
        if (i, by) not in rolled:
            rolled[i, by] = pltpu.roll(blocks[i], by, 1)
        return rolled[i, by]

    right = jnp.where(lane < 127, turned(m, 127), turned(m + 1, 127))
    return right + jnp.where(lane > 0, turned(m, 1), turned(m - 1, 1))


def parts(centre, ahead, behind, beside, half_z, half_y):
    up, down = pltpu.roll(centre, centre.shape[0] - 1, 0), pltpu.roll(centre, 1, 0)
    near = (ahead + behind) + (up + down) + beside
    return near - 6.0 * centre, half_z * (ahead - behind) + half_y * (up - down)


def rates(fuels, heats, kappa, vel_z, vel_y):
    half_z, half_y = 0.5 * vel_z, 0.5 * vel_y
    fuel_lap, fuel_adv = parts(*fuels, half_z, half_y)
    heat_lap, heat_adv = parts(*heats, half_z, half_y)
    square = heats[0] * heats[0]
    burning = burn_rate * fuels[0] * square / (1.0 + square)
    return (
        lewis_ratio * kappa * fuel_lap - fuel_adv - burning,
        kappa * heat_lap - heat_adv + heat_release * burning,
    )


def block_transpose(tiles):
    shape = (8, 128)
    row = lax.broadcasted_iota(jnp.int32, shape, 0)
    block = lax.broadcasted_iota(jnp.int32, shape, 1) // 16
    for bit in (4, 2, 1):
        row_bit, block_bit = (row & bit) != 0, (block & bit) != 0
        if bit == 4:
            moved = [pltpu.roll(pltpu.roll(tile, 64, 1), 4, 0) for tile in tiles]
        else:
            right = [pltpu.roll(tile, 16 * bit, 1) for tile in tiles]
            left = [pltpu.roll(tile, 128 - 16 * bit, 1) for tile in tiles]
            right = [pltpu.roll(tile, 8 - bit, 0) for tile in right]
            left = [pltpu.roll(tile, bit, 0) for tile in left]
            moved = [jnp.where(block_bit, r, l) for r, l in zip(right, left)]
        same = row_bit == block_bit
        tiles = [jnp.where(same, tile, other) for tile, other in zip(tiles, moved)]
    return tiles


def step_kernel(
    fuel, heat, kappa, vel_z, vel_y, low, high, outer, inner, out,
    halo, fuel_one, heat_one, heat_two, fuel_two, edge,
):
    planes, rows, size = fuel.shape
    columns = deep_planes((fuel, heat, kappa, vel_z, vel_y), low, high)

    def border(row_low, row_high):
        at = 0
        for j, (source, i, width) in enumerate(sum(columns, [])):
            halo[j, rows - width : rows] = row_low[at : at + width]
            halo[j, 0:width] = row_high[at : at + width]
            at += width

    odd = second_core()
    pl.when(odd)(lambda: border(inner, outer))
    pl.when(jnp.logical_not(odd))(lambda: border(outer, inner))

    parts_of = [slice(at, at + 128) for at in range(0, size, 128)]
    lane = lax.broadcasted_iota(jnp.int32, (2 * rows, 128), 1)

    def plane(field, j, m):
        source, i, width = columns[field][j]
        row = sum(len(column) for column in columns[:field]) + j
        return jnp.concatenate([source[i, :, parts_of[m]], halo[row, :, parts_of[m]]], axis=0)

    coupled = jnp.where(lax.axis_index("depth") > 0, 1.0, 0.0)

    for j in range(planes + 2):
        blocks = [[plane(f, j + 1, m) for m in range(len(parts_of))] for f in (0, 1)]
        rolled = ({}, {})
        for m, part in enumerate(parts_of):
            fuels, heats = (
                (
                    blocks[f][m],
                    plane(f, j + 2, m) * (coupled if j == 1 else 1.0),
                    plane(f, j, m) * (coupled if j == 2 else 1.0),
                    neighbours(blocks[f], m, lane, rolled[f]),
                )
                for f in (0, 1)
            )
            rate_fuel, rate_heat = rates(fuels, heats, *(plane(f, j, m) for f in (2, 3, 4)))
            fuel_one[j, :, part] = fuels[0] + time_step * rate_fuel
            heat_one[j, :, part] = heats[0] + time_step * rate_heat

    for j in range(planes):
        ones = (fuel_one, heat_one)
        blocks = [[ref[j + 1, :, part] for part in parts_of] for ref in ones]
        rolled = ({}, {})
        for m, part in enumerate(parts_of):
            fuels, heats = (
                (
                    blocks[f][m],
                    ones[f][j + 2, :, part] * (coupled if j == 0 else 1.0),
                    ones[f][j, :, part] * (coupled if j == 1 else 1.0),
                    neighbours(blocks[f], m, lane, rolled[f]),
                )
                for f in (0, 1)
            )
            rate_fuel, rate_heat = rates(fuels, heats, *(plane(f, j + 1, m) for f in (2, 3, 4)))
            final = 0.5 * (plane(0, j + 2, m) + fuels[0] + time_step * rate_fuel)
            fuel_two[j, :, part] = final[:rows]
            heat_two[j, :, part] = 0.5 * (plane(1, j + 2, m) + heats[0] + time_step * rate_heat)

    chunk = 2 * planes + 2
    count = size // 16

    def send(values, at):
        groups = size // 128
        tiles = [value[:, m * 128 : (m + 1) * 128] for value in values for m in range(groups)]
        for i, tile in enumerate(block_transpose(tiles)):
            row, m = at + i // groups, i % groups
            place = (8 * m - first_member(count)) % count
            before = min(8, count - place)
            out[pl.ds(place * chunk + row, before, stride=chunk), :] = tile[:before]
            if before < 8:
                out[pl.ds(row, 8 - before, stride=chunk), :] = tile[before:]

    lane = lax.broadcasted_iota(jnp.int32, (rows, size), 1)
    place = lane % 16
    borders = jnp.zeros((rows, size), jnp.float32)
    for p in range(planes):
        level = heat_two[p, :rows]
        send([level], p)
        send([fuel_two[p]], planes + p)
        edge[p : p + 1] = heat_two[p, 2 * rows - 1 : 2 * rows]
        edge[planes + p : planes + p + 1] = heat_two[p, rows : rows + 1]
        left = (place == p) & (lane >= 16)
        right = (place == planes + p) & (lane < size - 16)
        borders = jnp.where(left, pltpu.roll(level, p + 1, 1), borders)
        borders = jnp.where(right, pltpu.roll(level, size - 16 + planes + p, 1), borders)
    send([edge[...]], 2 * planes)
    send([borders], 2 * planes + 1)


def per_function(ref, *index):
    row = lax.broadcasted_iota(jnp.int32, (8, 128), 0)
    value = jnp.full((8, 128), ref[(0,) + index], jnp.float32)
    for k in range(1, 8):
        value = jnp.where(row == k, ref[(k,) + index], value)
    return value


def march_kernel(opacity_scale, planes, centre, width, density, tint, fields, out, lights):
    chunk = 2 * planes + 2
    count = fields.shape[0] // chunk
    columns = [fields[pl.ds(i, count, stride=chunk), :] for i in range(planes)]
    edge, borders = (
        fields[pl.ds(2 * planes + i, count, stride=chunk), :] for i in range(2)
    )
    lane = lax.broadcasted_iota(jnp.int32, (count, 128), 1)
    place = lane % 16
    row = lax.broadcasted_iota(jnp.int32, (count, 128), 0)
    coupled = row != (count - first_member(count)) % count
    for p in range(planes):
        level = columns[p]
        ahead = columns[p + 1] if p + 1 < planes else pltpu.roll(columns[0], count - 1, 0)
        behind = columns[p - 1] if p > 0 else pltpu.roll(columns[planes - 1], 1, 0)
        if p == 0:
            ahead = jnp.where(coupled, ahead, 0.0)
        if p == 1:
            behind = jnp.where(coupled, behind, 0.0)

        def moved(value, by):
            by = by % 128
            return pltpu.roll(value, by, 1) if by else value

        up = jnp.where(lane < 112, moved(level, -16), moved(edge, 112 - 16 * (planes + p)))
        down = jnp.where(lane >= 16, moved(level, 16), moved(edge, -16 * p))
        right = jnp.where(place < 15, moved(level, -1), moved(borders, 15 - planes - p))
        left = jnp.where(place > 0, moved(level, 1), moved(borders, -p))
        grad_z, grad_y, grad_x = 0.5 * (ahead - behind), 0.5 * (up - down), 0.5 * (right - left)
        norm_sq = grad_z * grad_z + grad_y * grad_y + grad_x * grad_x + 1.0
        facing = 0.48 * grad_z + 0.6 * grad_y + 0.64 * grad_x
        lights[p] = 0.5 * (0.35 + 0.65 * (facing * facing) / norm_sq)

    mid = per_function(centre)
    spread = per_function(width)
    narrow = -log2_e / (spread * spread)
    thick = per_function(density) * (-log2_e * opacity_scale)
    half = [0.5 * per_function(tint, c) for c in range(3)]

    def one_plane(at, s, p, state):
        passing, total, *colour = state
        level, fuel = fields[pl.ds(at + p, 1), :], fields[pl.ds(at + planes + p, 1), :]
        offset = level - mid
        survive = jnp.exp2(thick * jnp.exp2(narrow * (offset * offset)))
        left = passing * survive
        weight = (passing - left) * lights[p, pl.ds(s, 1)]
        colour = [value + weight * jnp.tanh(half[c] * fuel) for c, value in enumerate(colour)]
        return (left, total + weight, *colour)

    joint = 8

    def segments(i, state):
        for s in range(joint):
            s = i * joint + s + (count - first_member(count))
            now, after = lax.rem(s, count), lax.rem(s + 1, count)
            for p in range(1, planes):
                state = one_plane(now * chunk, now, p, state)
            state = one_plane(after * chunk, after, 0, state)
        return state

    zero = jnp.zeros((8, 128), jnp.float32)
    state = lax.fori_loop(0, count // joint, segments, (zero + 1.0, zero, zero, zero, zero))
    passing, total, *colour = state
    values = [total + value for value in colour] + [passing]
    for c, tile in enumerate(block_transpose(values)):
        for k in range(8):
            out[k, c] = tile[:, 16 * k : 16 * k + 16]


def body(fuel, heat, kappa, vel_z, vel_y, tf_centre, tf_width, tf_density, tf_tint):
    planes, rows, columns = fuel.shape
    depth_count = lax.axis_size("depth")
    fields = (fuel, heat, kappa, vel_z, vel_y)
    f32 = functools.partial(jax.ShapeDtypeStruct, dtype=jnp.float32)
    sent_rows = sum(planes * (1 + deep) + deep * (1 + deep) for deep in depths)

    to_next, to_prev = pl.pallas_call(
        planes_kernel,
        out_shape=[f32((sum(widths), rows, columns)) for widths in (befores, afters)],
        in_specs=[hbm] * 5,
        out_specs=[vmem] * 2,
        scratch_shapes=[pltpu.SemaphoreType.DMA((2 * len(depths),))],
        compiler_params=params(),
        name="pack_planes",
    )(*(pltpu.with_memory_space_constraint(field, pltpu.HBM) for field in fields))
    low, high = exchange(to_next, to_prev, "depth")
    outer, inner = pl.pallas_call(
        rows_kernel,
        out_shape=[f32((sent_rows, columns))] * 2,
        in_specs=[vmem] * 7,
        out_specs=[vmem] * 2,
        compiler_params=params(),
        name="pack_rows",
    )(*fields, low, high)
    outer, inner = swap(outer, "rows", 1), swap(inner, "rows", 0)

    chunk = 2 * planes + 2
    tall = 2 * rows
    deep_count = sum(planes + 2 * deep for deep in depths)
    scratch = [pltpu.VMEM((deep_count, rows, columns), jnp.float32)]
    scratch += [pltpu.VMEM((planes + 2, tall, columns), jnp.float32)] * 2
    scratch += [pltpu.VMEM((planes, tall, columns), jnp.float32)]
    scratch += [pltpu.VMEM((planes, rows, columns), jnp.float32)]
    scratch += [pltpu.VMEM((2 * planes, columns), jnp.float32)]
    stepped = pl.pallas_call(
        step_kernel,
        out_shape=f32((depth_count * chunk, 128)),
        in_specs=[vmem] * 9,
        out_specs=vmem,
        scratch_shapes=scratch,
        compiler_params=params(),
        name="step",
    )(*fields, low, high, outer, inner)

    order = [(first_member(depth_count) + i) % depth_count for i in range(depth_count)]
    gathered = lax.all_to_all(
        stepped.reshape(depth_count, 1, chunk * 128),
        "depth",
        split_axis=0,
        concat_axis=0,
        axis_index_groups=[order],
        tiled=True,
    ).reshape(depth_count * chunk, 128)

    return pl.pallas_call(
        functools.partial(march_kernel, 4.0 / (planes * depth_count), planes),
        out_shape=f32((8, 4, rows, columns // depth_count)),
        in_specs=[smem] * 4 + [vmem],
        out_specs=vmem,
        scratch_shapes=[pltpu.VMEM((planes, depth_count, 128), jnp.float32)],
        compiler_params=params(),
        name="march",
    )(tf_centre, tf_width, tf_density, tf_tint, gathered)


def solution(mesh):
    placed = (P("depth", "rows", None),) * 5 + (P(),) * 4
    return jax.shard_map(
        body, mesh=mesh, in_specs=placed, out_specs=P(None, None, "rows", "depth"), check_vma=False
    )
```

```python
import functools
import math

import jax
import jax.numpy as jnp
from jax import lax
from jax.experimental import pallas as pl
from jax.experimental.pallas import tpu as pltpu
from jax.sharding import PartitionSpec as P

time_step = 1.0
lewis_ratio = 0.8
heat_release = 0.6
burn_rate = 0.5

befores = (3, 3, 2, 2, 2)
afters = (1, 1, 0, 0, 0)
depths = (2, 2, 1, 1, 1)
log2_e = math.log2(math.e)

vmem = pl.BlockSpec(memory_space=pltpu.VMEM)
smem = pl.BlockSpec(memory_space=pltpu.SMEM)
hbm = pl.BlockSpec(memory_space=pltpu.HBM)


def first_member(count):
    return 5 * count // 8


def exchange(to_next, to_prev, axis):
    count = lax.axis_size(axis)
    forward = [(i, (i + 1) % count) for i in range(count)]
    backward = [(i + 1, i) for i in range(count - 1)]
    return lax.ppermute(to_next, axis, forward), lax.ppermute(to_prev, axis, backward)


def swap(block, axis, first):
    count = lax.axis_size(axis)
    forward = [(i, i + 1) for i in range(first, count - 1, 2)]
    return lax.ppermute(block, axis, forward + [(target, source) for source, target in forward])


def second_core():
    return lax.rem(lax.axis_index("rows"), 2) == 1


def params(**more):
    return pltpu.CompilerParams(vmem_limit_bytes=8 << 20, **more)


def planes_kernel(fuel, heat, kappa, vel_z, vel_y, to_next, to_prev, arrived):
    planes = fuel.shape[0]
    fields = (fuel, heat, kappa, vel_z, vel_y)
    copies = []
    for target, widths, last in ((to_next, befores, True), (to_prev, afters, False)):
        at = 0
        for field, width in zip(fields, widths):
            if width:
                source = field.at[pl.ds(planes - width if last else 0, width)]
                copies.append((source, target.at[pl.ds(at, width)]))
            at += width
    copies = [
        pltpu.make_async_copy(source, target, arrived.at[i])
        for i, (source, target) in enumerate(copies)
    ]
    for copy in copies:
        copy.start()
    for copy in copies:
        copy.wait()


def deep_planes(fields, low, high):
    planes = fields[0].shape[0]
    at_low = at_high = 0
    columns = []
    for field, before, after, deep in zip(fields, befores, afters, depths):
        column = [(low, at_low + i) for i in range(before)]
        column += [(field, i) for i in range(planes)]
        column += [(high, at_high + i) for i in range(after)]
        last = len(column) - 1
        columns.append(
            [(*plane, 1 + min(deep, j, last - j)) for j, plane in enumerate(column)]
        )
        at_low, at_high = at_low + before, at_high + after
    return columns


def rows_kernel(fuel, heat, kappa, vel_z, vel_y, low, high, outer, inner):
    rows = fuel.shape[1]
    columns = deep_planes((fuel, heat, kappa, vel_z, vel_y), low, high)

    def fill(to_next, to_prev):
        at = 0
        for column in columns:
            for source, i, width in column:
                to_next[at : at + width] = source[i, rows - width : rows]
                to_prev[at : at + width] = source[i, 0:width]
                at += width

    odd = second_core()
    pl.when(odd)(lambda: fill(outer, inner))
    pl.when(jnp.logical_not(odd))(lambda: fill(inner, outer))


def neighbours(blocks, m, lane, rolled):
    def turned(i, by):
        if not 0 <= i < len(blocks):
            return 0.0
        if (i, by) not in rolled:
            rolled[i, by] = pltpu.roll(blocks[i], by, 1)
        return rolled[i, by]

    right = jnp.where(lane < 127, turned(m, 127), turned(m + 1, 127))
    return right + jnp.where(lane > 0, turned(m, 1), turned(m - 1, 1))


def parts(centre, ahead, behind, beside, half_z, half_y):
    up, down = pltpu.roll(centre, centre.shape[0] - 1, 0), pltpu.roll(centre, 1, 0)
    near = (ahead + behind) + (up + down) + beside
    return near - 6.0 * centre, half_z * (ahead - behind) + half_y * (up - down)


def rates(fuels, heats, kappa, vel_z, vel_y):
    half_z, half_y = 0.5 * vel_z, 0.5 * vel_y
    fuel_lap, fuel_adv = parts(*fuels, half_z, half_y)
    heat_lap, heat_adv = parts(*heats, half_z, half_y)
    square = heats[0] * heats[0]
    burning = burn_rate * fuels[0] * square / (1.0 + square)
    return (
        lewis_ratio * kappa * fuel_lap - fuel_adv - burning,
        kappa * heat_lap - heat_adv + heat_release * burning,
    )


def block_transpose(tiles):
    shape = (8, 128)
    row = lax.broadcasted_iota(jnp.int32, shape, 0)
    block = lax.broadcasted_iota(jnp.int32, shape, 1) // 16
    for bit in (4, 2, 1):
        row_bit, block_bit = (row & bit) != 0, (block & bit) != 0
        if bit == 4:
            moved = [pltpu.roll(pltpu.roll(tile, 64, 1), 4, 0) for tile in tiles]
        else:
            right = [pltpu.roll(tile, 16 * bit, 1) for tile in tiles]
            left = [pltpu.roll(tile, 128 - 16 * bit, 1) for tile in tiles]
            right = [pltpu.roll(tile, 8 - bit, 0) for tile in right]
            left = [pltpu.roll(tile, bit, 0) for tile in left]
            moved = [jnp.where(block_bit, r, l) for r, l in zip(right, left)]
        same = row_bit == block_bit
        tiles = [jnp.where(same, tile, other) for tile, other in zip(tiles, moved)]
    return tiles


def step_kernel(
    fuel, heat, kappa, vel_z, vel_y, low, high, outer, inner, out,
    halo, fuel_one, heat_one, heat_two, fuel_two, edge,
):
    planes, rows, size = fuel.shape
    columns = deep_planes((fuel, heat, kappa, vel_z, vel_y), low, high)

    def border(row_low, row_high):
        at = 0
        for j, (source, i, width) in enumerate(sum(columns, [])):
            halo[j, rows - width : rows] = row_low[at : at + width]
            halo[j, 0:width] = row_high[at : at + width]
            at += width

    odd = second_core()
    pl.when(odd)(lambda: border(inner, outer))
    pl.when(jnp.logical_not(odd))(lambda: border(outer, inner))

    parts_of = [slice(at, at + 128) for at in range(0, size, 128)]
    lane = lax.broadcasted_iota(jnp.int32, (2 * rows, 128), 1)

    def plane(field, j, m):
        source, i, width = columns[field][j]
        row = sum(len(column) for column in columns[:field]) + j
        return jnp.concatenate([source[i, :, parts_of[m]], halo[row, :, parts_of[m]]], axis=0)

    coupled = jnp.where(lax.axis_index("depth") > 0, 1.0, 0.0)

    for j in range(planes + 2):
        blocks = [[plane(f, j + 1, m) for m in range(len(parts_of))] for f in (0, 1)]
        rolled = ({}, {})
        for m, part in enumerate(parts_of):
            fuels, heats = (
                (
                    blocks[f][m],
                    plane(f, j + 2, m) * (coupled if j == 1 else 1.0),
                    plane(f, j, m) * (coupled if j == 2 else 1.0),
                    neighbours(blocks[f], m, lane, rolled[f]),
                )
                for f in (0, 1)
            )
            rate_fuel, rate_heat = rates(fuels, heats, *(plane(f, j, m) for f in (2, 3, 4)))
            fuel_one[j, :, part] = fuels[0] + time_step * rate_fuel
            heat_one[j, :, part] = heats[0] + time_step * rate_heat

    for j in range(planes):
        ones = (fuel_one, heat_one)
        blocks = [[ref[j + 1, :, part] for part in parts_of] for ref in ones]
        rolled = ({}, {})
        for m, part in enumerate(parts_of):
            fuels, heats = (
                (
                    blocks[f][m],
                    ones[f][j + 2, :, part] * (coupled if j == 0 else 1.0),
                    ones[f][j, :, part] * (coupled if j == 1 else 1.0),
                    neighbours(blocks[f], m, lane, rolled[f]),
                )
                for f in (0, 1)
            )
            rate_fuel, rate_heat = rates(fuels, heats, *(plane(f, j + 1, m) for f in (2, 3, 4)))
            final = 0.5 * (plane(0, j + 2, m) + fuels[0] + time_step * rate_fuel)
            fuel_two[j, :, part] = final[:rows]
            heat_two[j, :, part] = 0.5 * (plane(1, j + 2, m) + heats[0] + time_step * rate_heat)

    chunk = 2 * planes + 2
    count = size // 16

    def send(values, at):
        groups = size // 128
        tiles = [value[:, m * 128 : (m + 1) * 128] for value in values for m in range(groups)]
        for i, tile in enumerate(block_transpose(tiles)):
            row, m = at + i // groups, i % groups
            place = (8 * m - first_member(count)) % count
            before = min(8, count - place)
            out[pl.ds(place * chunk + row, before, stride=chunk), :] = tile[:before]
            if before < 8:
                out[pl.ds(row, 8 - before, stride=chunk), :] = tile[before:]

    lane = lax.broadcasted_iota(jnp.int32, (rows, size), 1)
    place = lane % 16
    borders = jnp.zeros((rows, size), jnp.float32)
    for p in range(planes):
        level = heat_two[p, :rows]
        send([level], p)
        send([fuel_two[p]], planes + p)
        edge[p : p + 1] = heat_two[p, 2 * rows - 1 : 2 * rows]
        edge[planes + p : planes + p + 1] = heat_two[p, rows : rows + 1]
        left = (place == p) & (lane >= 16)
        right = (place == planes + p) & (lane < size - 16)
        borders = jnp.where(left, pltpu.roll(level, p + 1, 1), borders)
        borders = jnp.where(right, pltpu.roll(level, size - 16 + planes + p, 1), borders)
    send([edge[...]], 2 * planes)
    send([borders], 2 * planes + 1)


def per_function(ref, *index):
    row = lax.broadcasted_iota(jnp.int32, (8, 128), 0)
    value = jnp.full((8, 128), ref[(0,) + index], jnp.float32)
    for k in range(1, 8):
        value = jnp.where(row == k, ref[(k,) + index], value)
    return value


def functions_kernel(opacity_scale, centre, width, density, tint, out):
    spread = per_function(width)
    out[0] = per_function(centre)
    out[1] = -log2_e / (spread * spread)
    out[2] = per_function(density) * (-log2_e * opacity_scale)
    for c in range(3):
        out[3 + c] = 0.5 * per_function(tint, c)


def march_kernel(planes, functions, fields, out, lights):
    chunk = 2 * planes + 2
    count = fields.shape[0] // chunk
    columns = [fields[pl.ds(i, count, stride=chunk), :] for i in range(planes)]
    edge, borders = (
        fields[pl.ds(2 * planes + i, count, stride=chunk), :] for i in range(2)
    )
    lane = lax.broadcasted_iota(jnp.int32, (count, 128), 1)
    place = lane % 16
    row = lax.broadcasted_iota(jnp.int32, (count, 128), 0)
    coupled = row != (count - first_member(count)) % count
    for p in range(planes):
        level = columns[p]
        ahead = columns[p + 1] if p + 1 < planes else pltpu.roll(columns[0], count - 1, 0)
        behind = columns[p - 1] if p > 0 else pltpu.roll(columns[planes - 1], 1, 0)
        if p == 0:
            ahead = jnp.where(coupled, ahead, 0.0)
        if p == 1:
            behind = jnp.where(coupled, behind, 0.0)

        def moved(value, by):
            by = by % 128
            return pltpu.roll(value, by, 1) if by else value

        up = jnp.where(lane < 112, moved(level, -16), moved(edge, 112 - 16 * (planes + p)))
        down = jnp.where(lane >= 16, moved(level, 16), moved(edge, -16 * p))
        right = jnp.where(place < 15, moved(level, -1), moved(borders, 15 - planes - p))
        left = jnp.where(place > 0, moved(level, 1), moved(borders, -p))
        grad_z, grad_y, grad_x = 0.5 * (ahead - behind), 0.5 * (up - down), 0.5 * (right - left)
        norm_sq = grad_z * grad_z + grad_y * grad_y + grad_x * grad_x + 1.0
        facing = 0.48 * grad_z + 0.6 * grad_y + 0.64 * grad_x
        lights[p] = 0.5 * (0.35 + 0.65 * (facing * facing) / norm_sq)

    mid, narrow, thick, *half = (functions[i] for i in range(6))

    def one_plane(at, s, p, state):
        passing, total, *colour = state
        level, fuel = fields[pl.ds(at + p, 1), :], fields[pl.ds(at + planes + p, 1), :]
        offset = level - mid
        survive = jnp.exp2(thick * jnp.exp2(narrow * (offset * offset)))
        left = passing * survive
        weight = (passing - left) * lights[p, pl.ds(s, 1)]
        colour = [value + weight * jnp.tanh(half[c] * fuel) for c, value in enumerate(colour)]
        return (left, total + weight, *colour)

    joint = 8

    def segments(i, state):
        for s in range(joint):
            s = i * joint + s + (count - first_member(count))
            now, after = lax.rem(s, count), lax.rem(s + 1, count)
            for p in range(1, planes):
                state = one_plane(now * chunk, now, p, state)
            state = one_plane(after * chunk, after, 0, state)
        return state

    zero = jnp.zeros((8, 128), jnp.float32)
    state = lax.fori_loop(0, count // joint, segments, (zero + 1.0, zero, zero, zero, zero))
    passing, total, *colour = state
    values = [total + value for value in colour] + [passing]
    for c, tile in enumerate(block_transpose(values)):
        for k in range(8):
            out[k, c] = tile[:, 16 * k : 16 * k + 16]


def body(fuel, heat, kappa, vel_z, vel_y, tf_centre, tf_width, tf_density, tf_tint):
    planes, rows, columns = fuel.shape
    depth_count = lax.axis_size("depth")
    fields = (fuel, heat, kappa, vel_z, vel_y)
    f32 = functools.partial(jax.ShapeDtypeStruct, dtype=jnp.float32)
    sent_rows = sum(planes * (1 + deep) + deep * (1 + deep) for deep in depths)

    to_next, to_prev = pl.pallas_call(
        planes_kernel,
        out_shape=[f32((sum(widths), rows, columns)) for widths in (befores, afters)],
        in_specs=[hbm] * 5,
        out_specs=[vmem] * 2,
        scratch_shapes=[pltpu.SemaphoreType.DMA((2 * len(depths),))],
        compiler_params=params(),
        name="pack_planes",
    )(*(pltpu.with_memory_space_constraint(field, pltpu.HBM) for field in fields))
    low, high = exchange(to_next, to_prev, "depth")
    outer, inner = pl.pallas_call(
        rows_kernel,
        out_shape=[f32((sent_rows, columns))] * 2,
        in_specs=[vmem] * 7,
        out_specs=[vmem] * 2,
        compiler_params=params(),
        name="pack_rows",
    )(*fields, low, high)
    outer, inner = swap(outer, "rows", 1), swap(inner, "rows", 0)

    chunk = 2 * planes + 2
    tall = 2 * rows
    deep_count = sum(planes + 2 * deep for deep in depths)
    scratch = [pltpu.VMEM((deep_count, rows, columns), jnp.float32)]
    scratch += [pltpu.VMEM((planes + 2, tall, columns), jnp.float32)] * 2
    scratch += [pltpu.VMEM((planes, tall, columns), jnp.float32)]
    scratch += [pltpu.VMEM((planes, rows, columns), jnp.float32)]
    scratch += [pltpu.VMEM((2 * planes, columns), jnp.float32)]
    stepped = pl.pallas_call(
        step_kernel,
        out_shape=f32((depth_count * chunk, 128)),
        in_specs=[vmem] * 9,
        out_specs=vmem,
        scratch_shapes=scratch,
        compiler_params=params(),
        name="step",
    )(*fields, low, high, outer, inner)

    order = [(first_member(depth_count) + i) % depth_count for i in range(depth_count)]
    gathered = lax.all_to_all(
        stepped.reshape(depth_count, 1, chunk * 128),
        "depth",
        split_axis=0,
        concat_axis=0,
        axis_index_groups=[order],
        tiled=True,
    ).reshape(depth_count * chunk, 128)

    functions = pl.pallas_call(
        functools.partial(functions_kernel, 4.0 / (planes * depth_count)),
        out_shape=f32((6, 8, 128)),
        in_specs=[smem] * 4,
        out_specs=vmem,
        compiler_params=params(),
        name="functions",
    )(tf_centre, tf_width, tf_density, tf_tint)

    return pl.pallas_call(
        functools.partial(march_kernel, planes),
        out_shape=f32((8, 4, rows, columns // depth_count)),
        in_specs=[vmem] * 2,
        out_specs=vmem,
        scratch_shapes=[pltpu.VMEM((planes, depth_count, 128), jnp.float32)],
        compiler_params=params(),
        name="march",
    )(functions, gathered)


def solution(mesh):
    placed = (P("depth", "rows", None),) * 5 + (P(),) * 4
    return jax.shard_map(
        body, mesh=mesh, in_specs=placed, out_specs=P(None, None, "rows", "depth"), check_vma=False
    )
```

```python
import functools
import math

import jax
import jax.numpy as jnp
from jax import lax
from jax.experimental import pallas as pl
from jax.experimental.pallas import tpu as pltpu
from jax.sharding import PartitionSpec as P

time_step = 1.0
lewis_ratio = 0.8
heat_release = 0.6
burn_rate = 0.5

befores = (3, 3, 2, 2, 2)
afters = (1, 1, 0, 0, 0)
depths = (2, 2, 1, 1, 1)
log2_e = math.log2(math.e)

vmem = pl.BlockSpec(memory_space=pltpu.VMEM)
smem = pl.BlockSpec(memory_space=pltpu.SMEM)
hbm = pl.BlockSpec(memory_space=pltpu.HBM)


def member_order(count):
    root = 5 * count // 8
    return [root] + [i for i in range(count) if i != root]


def exchange(to_next, to_prev, axis):
    count = lax.axis_size(axis)
    forward = [(i, (i + 1) % count) for i in range(count)]
    backward = [(i + 1, i) for i in range(count - 1)]
    return lax.ppermute(to_next, axis, forward), lax.ppermute(to_prev, axis, backward)


def swap(block, axis, first):
    count = lax.axis_size(axis)
    forward = [(i, i + 1) for i in range(first, count - 1, 2)]
    return lax.ppermute(block, axis, forward + [(target, source) for source, target in forward])


def second_core():
    return lax.rem(lax.axis_index("rows"), 2) == 1


def params(**more):
    return pltpu.CompilerParams(vmem_limit_bytes=8 << 20, **more)


def planes_kernel(fuel, heat, kappa, vel_z, vel_y, to_next, to_prev, arrived):
    planes = fuel.shape[0]
    fields = (fuel, heat, kappa, vel_z, vel_y)
    copies = []
    for target, widths, last in ((to_next, befores, True), (to_prev, afters, False)):
        at = 0
        for field, width in zip(fields, widths):
            if width:
                source = field.at[pl.ds(planes - width if last else 0, width)]
                copies.append((source, target.at[pl.ds(at, width)]))
            at += width
    copies = [
        pltpu.make_async_copy(source, target, arrived.at[i])
        for i, (source, target) in enumerate(copies)
    ]
    for copy in copies:
        copy.start()
    for copy in copies:
        copy.wait()


def deep_planes(fields, low, high):
    planes = fields[0].shape[0]
    at_low = at_high = 0
    columns = []
    for field, before, after, deep in zip(fields, befores, afters, depths):
        column = [(low, at_low + i) for i in range(before)]
        column += [(field, i) for i in range(planes)]
        column += [(high, at_high + i) for i in range(after)]
        last = len(column) - 1
        columns.append(
            [(*plane, 1 + min(deep, j, last - j)) for j, plane in enumerate(column)]
        )
        at_low, at_high = at_low + before, at_high + after
    return columns


def rows_kernel(fuel, heat, kappa, vel_z, vel_y, low, high, outer, inner):
    rows = fuel.shape[1]
    columns = deep_planes((fuel, heat, kappa, vel_z, vel_y), low, high)

    def fill(to_next, to_prev):
        at = 0
        for column in columns:
            for source, i, width in column:
                to_next[at : at + width] = source[i, rows - width : rows]
                to_prev[at : at + width] = source[i, 0:width]
                at += width

    odd = second_core()
    pl.when(odd)(lambda: fill(outer, inner))
    pl.when(jnp.logical_not(odd))(lambda: fill(inner, outer))


def neighbours(blocks, m, lane, rolled):
    def turned(i, by):
        if not 0 <= i < len(blocks):
            return 0.0
        if (i, by) not in rolled:
            rolled[i, by] = pltpu.roll(blocks[i], by, 1)
        return rolled[i, by]

    right = jnp.where(lane < 127, turned(m, 127), turned(m + 1, 127))
    return right + jnp.where(lane > 0, turned(m, 1), turned(m - 1, 1))


def parts(centre, ahead, behind, beside, half_z, half_y):
    up, down = pltpu.roll(centre, centre.shape[0] - 1, 0), pltpu.roll(centre, 1, 0)
    near = (ahead + behind) + (up + down) + beside
    return near - 6.0 * centre, half_z * (ahead - behind) + half_y * (up - down)


def rates(fuels, heats, kappa, vel_z, vel_y):
    half_z, half_y = 0.5 * vel_z, 0.5 * vel_y
    fuel_lap, fuel_adv = parts(*fuels, half_z, half_y)
    heat_lap, heat_adv = parts(*heats, half_z, half_y)
    square = heats[0] * heats[0]
    burning = burn_rate * fuels[0] * square / (1.0 + square)
    return (
        lewis_ratio * kappa * fuel_lap - fuel_adv - burning,
        kappa * heat_lap - heat_adv + heat_release * burning,
    )


def block_transpose(tiles):
    shape = (8, 128)
    row = lax.broadcasted_iota(jnp.int32, shape, 0)
    block = lax.broadcasted_iota(jnp.int32, shape, 1) // 16
    for bit in (4, 2, 1):
        row_bit, block_bit = (row & bit) != 0, (block & bit) != 0
        if bit == 4:
            moved = [pltpu.roll(pltpu.roll(tile, 64, 1), 4, 0) for tile in tiles]
        else:
            right = [pltpu.roll(tile, 16 * bit, 1) for tile in tiles]
            left = [pltpu.roll(tile, 128 - 16 * bit, 1) for tile in tiles]
            right = [pltpu.roll(tile, 8 - bit, 0) for tile in right]
            left = [pltpu.roll(tile, bit, 0) for tile in left]
            moved = [jnp.where(block_bit, r, l) for r, l in zip(right, left)]
        same = row_bit == block_bit
        tiles = [jnp.where(same, tile, other) for tile, other in zip(tiles, moved)]
    return tiles


def step_kernel(
    fuel, heat, kappa, vel_z, vel_y, low, high, outer, inner, out,
    halo, fuel_one, heat_one, heat_two, fuel_two, edge,
):
    planes, rows, size = fuel.shape
    columns = deep_planes((fuel, heat, kappa, vel_z, vel_y), low, high)

    def border(row_low, row_high):
        at = 0
        for j, (source, i, width) in enumerate(sum(columns, [])):
            halo[j, rows - width : rows] = row_low[at : at + width]
            halo[j, 0:width] = row_high[at : at + width]
            at += width

    odd = second_core()
    pl.when(odd)(lambda: border(inner, outer))
    pl.when(jnp.logical_not(odd))(lambda: border(outer, inner))

    parts_of = [slice(at, at + 128) for at in range(0, size, 128)]
    lane = lax.broadcasted_iota(jnp.int32, (2 * rows, 128), 1)

    def plane(field, j, m):
        source, i, width = columns[field][j]
        row = sum(len(column) for column in columns[:field]) + j
        return jnp.concatenate([source[i, :, parts_of[m]], halo[row, :, parts_of[m]]], axis=0)

    coupled = jnp.where(lax.axis_index("depth") > 0, 1.0, 0.0)

    for j in range(planes + 2):
        blocks = [[plane(f, j + 1, m) for m in range(len(parts_of))] for f in (0, 1)]
        rolled = ({}, {})
        for m, part in enumerate(parts_of):
            fuels, heats = (
                (
                    blocks[f][m],
                    plane(f, j + 2, m) * (coupled if j == 1 else 1.0),
                    plane(f, j, m) * (coupled if j == 2 else 1.0),
                    neighbours(blocks[f], m, lane, rolled[f]),
                )
                for f in (0, 1)
            )
            rate_fuel, rate_heat = rates(fuels, heats, *(plane(f, j, m) for f in (2, 3, 4)))
            fuel_one[j, :, part] = fuels[0] + time_step * rate_fuel
            heat_one[j, :, part] = heats[0] + time_step * rate_heat

    for j in range(planes):
        ones = (fuel_one, heat_one)
        blocks = [[ref[j + 1, :, part] for part in parts_of] for ref in ones]
        rolled = ({}, {})
        for m, part in enumerate(parts_of):
            fuels, heats = (
                (
                    blocks[f][m],
                    ones[f][j + 2, :, part] * (coupled if j == 0 else 1.0),
                    ones[f][j, :, part] * (coupled if j == 1 else 1.0),
                    neighbours(blocks[f], m, lane, rolled[f]),
                )
                for f in (0, 1)
            )
            rate_fuel, rate_heat = rates(fuels, heats, *(plane(f, j + 1, m) for f in (2, 3, 4)))
            final = 0.5 * (plane(0, j + 2, m) + fuels[0] + time_step * rate_fuel)
            fuel_two[j, :, part] = final[:rows]
            heat_two[j, :, part] = 0.5 * (plane(1, j + 2, m) + heats[0] + time_step * rate_heat)

    chunk = 2 * planes + 2
    count = size // 16
    order = member_order(count)

    def send(values, at):
        groups = size // 128
        tiles = [value[:, m * 128 : (m + 1) * 128] for value in values for m in range(groups)]
        for i, tile in enumerate(block_transpose(tiles)):
            row, m = at + i // groups, i % groups
            places = [order.index(8 * m + l) for l in range(8)]
            cuts = [l for l in range(1, 8) if places[l] != places[l - 1] + 1]
            for start, end in zip([0] + cuts, cuts + [8]):
                owners = pl.ds(places[start] * chunk + row, end - start, stride=chunk)
                out[owners, :] = tile[start:end]

    lane = lax.broadcasted_iota(jnp.int32, (rows, size), 1)
    place = lane % 16
    borders = jnp.zeros((rows, size), jnp.float32)
    for p in range(planes):
        level = heat_two[p, :rows]
        send([level], p)
        send([fuel_two[p]], planes + p)
        edge[p : p + 1] = heat_two[p, 2 * rows - 1 : 2 * rows]
        edge[planes + p : planes + p + 1] = heat_two[p, rows : rows + 1]
        left = (place == p) & (lane >= 16)
        right = (place == planes + p) & (lane < size - 16)
        borders = jnp.where(left, pltpu.roll(level, p + 1, 1), borders)
        borders = jnp.where(right, pltpu.roll(level, size - 16 + planes + p, 1), borders)
    send([edge[...]], 2 * planes)
    send([borders], 2 * planes + 1)


def per_function(ref, *index):
    row = lax.broadcasted_iota(jnp.int32, (8, 128), 0)
    value = jnp.full((8, 128), ref[(0,) + index], jnp.float32)
    for k in range(1, 8):
        value = jnp.where(row == k, ref[(k,) + index], value)
    return value


def functions_kernel(opacity_scale, centre, width, density, tint, out):
    spread = per_function(width)
    out[0] = per_function(centre)
    out[1] = -log2_e / (spread * spread)
    out[2] = per_function(density) * (-log2_e * opacity_scale)
    for c in range(3):
        out[3 + c] = 0.5 * per_function(tint, c)


def march_kernel(planes, functions, fields, out, lights):
    chunk = 2 * planes + 2
    count = fields.shape[0] // chunk
    columns = [fields[pl.ds(i, count, stride=chunk), :] for i in range(planes)]
    edge, borders = (
        fields[pl.ds(2 * planes + i, count, stride=chunk), :] for i in range(2)
    )
    lane = lax.broadcasted_iota(jnp.int32, (count, 128), 1)
    place = lane % 16
    row = lax.broadcasted_iota(jnp.int32, (count, 128), 0)
    order = member_order(count)
    root = order[0]

    def segment(value, step):
        value_of = pltpu.roll(value, -step % count, 0)
        for s in (root - 1, root, root + 1, 0, count - 1):
            here, there = order.index(s), order.index((s + step) % count)
            if there != (here + step) % count:
                value_of = jnp.where(row == here, value[there : there + 1], value_of)
        return value_of

    coupled = row != order.index(0)
    for p in range(planes):
        level = columns[p]
        ahead = columns[p + 1] if p + 1 < planes else segment(columns[0], 1)
        behind = columns[p - 1] if p > 0 else segment(columns[planes - 1], -1)
        if p == 0:
            ahead = jnp.where(coupled, ahead, 0.0)
        if p == 1:
            behind = jnp.where(coupled, behind, 0.0)

        def moved(value, by):
            by = by % 128
            return pltpu.roll(value, by, 1) if by else value

        up = jnp.where(lane < 112, moved(level, -16), moved(edge, 112 - 16 * (planes + p)))
        down = jnp.where(lane >= 16, moved(level, 16), moved(edge, -16 * p))
        right = jnp.where(place < 15, moved(level, -1), moved(borders, 15 - planes - p))
        left = jnp.where(place > 0, moved(level, 1), moved(borders, -p))
        grad_z, grad_y, grad_x = 0.5 * (ahead - behind), 0.5 * (up - down), 0.5 * (right - left)
        norm_sq = grad_z * grad_z + grad_y * grad_y + grad_x * grad_x + 1.0
        facing = 0.48 * grad_z + 0.6 * grad_y + 0.64 * grad_x
        lights[p] = 0.5 * (0.35 + 0.65 * (facing * facing) / norm_sq)

    mid, narrow, thick, *half = (functions[i] for i in range(6))

    def one_plane(at, s, p, state):
        passing, total, *colour = state
        level, fuel = fields[pl.ds(at + p, 1), :], fields[pl.ds(at + planes + p, 1), :]
        offset = level - mid
        survive = jnp.exp2(thick * jnp.exp2(narrow * (offset * offset)))
        left = passing * survive
        weight = (passing - left) * lights[p, pl.ds(s, 1)]
        colour = [value + weight * jnp.tanh(half[c] * fuel) for c, value in enumerate(colour)]
        return (left, total + weight, *colour)

    joint = 8

    def place_of(s):
        return jnp.where(s == root, 0, jnp.where(s < root, s + 1, s))

    def segments(i, state):
        for s in range(joint):
            s = i * joint + s
            now, after = place_of(s), place_of(lax.rem(s + 1, count))
            for p in range(1, planes):
                state = one_plane(now * chunk, now, p, state)
            state = one_plane(after * chunk, after, 0, state)
        return state

    zero = jnp.zeros((8, 128), jnp.float32)
    state = lax.fori_loop(0, count // joint, segments, (zero + 1.0, zero, zero, zero, zero))
    passing, total, *colour = state
    values = [total + value for value in colour] + [passing]
    for c, tile in enumerate(block_transpose(values)):
        for k in range(8):
            out[k, c] = tile[:, 16 * k : 16 * k + 16]


def body(fuel, heat, kappa, vel_z, vel_y, tf_centre, tf_width, tf_density, tf_tint):
    planes, rows, columns = fuel.shape
    depth_count = lax.axis_size("depth")
    fields = (fuel, heat, kappa, vel_z, vel_y)
    f32 = functools.partial(jax.ShapeDtypeStruct, dtype=jnp.float32)
    sent_rows = sum(planes * (1 + deep) + deep * (1 + deep) for deep in depths)

    to_next, to_prev = pl.pallas_call(
        planes_kernel,
        out_shape=[f32((sum(widths), rows, columns)) for widths in (befores, afters)],
        in_specs=[hbm] * 5,
        out_specs=[vmem] * 2,
        scratch_shapes=[pltpu.SemaphoreType.DMA((2 * len(depths),))],
        compiler_params=params(),
        name="pack_planes",
    )(*(pltpu.with_memory_space_constraint(field, pltpu.HBM) for field in fields))
    low, high = exchange(to_next, to_prev, "depth")
    outer, inner = pl.pallas_call(
        rows_kernel,
        out_shape=[f32((sent_rows, columns))] * 2,
        in_specs=[vmem] * 7,
        out_specs=[vmem] * 2,
        compiler_params=params(),
        name="pack_rows",
    )(*fields, low, high)
    outer, inner = swap(outer, "rows", 1), swap(inner, "rows", 0)

    chunk = 2 * planes + 2
    tall = 2 * rows
    deep_count = sum(planes + 2 * deep for deep in depths)
    scratch = [pltpu.VMEM((deep_count, rows, columns), jnp.float32)]
    scratch += [pltpu.VMEM((planes + 2, tall, columns), jnp.float32)] * 2
    scratch += [pltpu.VMEM((planes, tall, columns), jnp.float32)]
    scratch += [pltpu.VMEM((planes, rows, columns), jnp.float32)]
    scratch += [pltpu.VMEM((2 * planes, columns), jnp.float32)]
    stepped = pl.pallas_call(
        step_kernel,
        out_shape=f32((depth_count * chunk, 128)),
        in_specs=[vmem] * 9,
        out_specs=vmem,
        scratch_shapes=scratch,
        compiler_params=params(),
        name="step",
    )(*fields, low, high, outer, inner)

    gathered = lax.all_to_all(
        stepped.reshape(depth_count, 1, chunk * 128),
        "depth",
        split_axis=0,
        concat_axis=0,
        axis_index_groups=[member_order(depth_count)],
        tiled=True,
    ).reshape(depth_count * chunk, 128)

    functions = pl.pallas_call(
        functools.partial(functions_kernel, 4.0 / (planes * depth_count)),
        out_shape=f32((6, 8, 128)),
        in_specs=[smem] * 4,
        out_specs=vmem,
        compiler_params=params(),
        name="functions",
    )(tf_centre, tf_width, tf_density, tf_tint)

    return pl.pallas_call(
        functools.partial(march_kernel, planes),
        out_shape=f32((8, 4, rows, columns // depth_count)),
        in_specs=[vmem] * 2,
        out_specs=vmem,
        scratch_shapes=[pltpu.VMEM((planes, depth_count, 128), jnp.float32)],
        compiler_params=params(),
        name="march",
    )(functions, gathered)


def solution(mesh):
    placed = (P("depth", "rows", None),) * 5 + (P(),) * 4
    return jax.shard_map(
        body, mesh=mesh, in_specs=placed, out_specs=P(None, None, "rows", "depth"), check_vma=False
    )
```

```python
import functools
import math

import jax
import jax.numpy as jnp
from jax import lax
from jax.experimental import pallas as pl
from jax.experimental.pallas import tpu as pltpu
from jax.sharding import PartitionSpec as P

time_step = 1.0
lewis_ratio = 0.8
heat_release = 0.6
burn_rate = 0.5

befores = (3, 3, 2, 2, 2)
afters = (1, 1, 0, 0, 0)
depths = (2, 2, 1, 1, 1)
log2_e = math.log2(math.e)

vmem = pl.BlockSpec(memory_space=pltpu.VMEM)
smem = pl.BlockSpec(memory_space=pltpu.SMEM)
hbm = pl.BlockSpec(memory_space=pltpu.HBM)


def first_member(count):
    return 5 * count // 8


def exchange(to_next, to_prev, axis):
    count = lax.axis_size(axis)
    forward = [(i, (i + 1) % count) for i in range(count)]
    backward = [(i + 1, i) for i in range(count - 1)]
    return lax.ppermute(to_next, axis, forward), lax.ppermute(to_prev, axis, backward)


def swap(block, axis, first):
    count = lax.axis_size(axis)
    forward = [(i, i + 1) for i in range(first, count - 1, 2)]
    return lax.ppermute(block, axis, forward + [(target, source) for source, target in forward])


def second_core():
    return lax.rem(lax.axis_index("rows"), 2) == 1


def params(**more):
    return pltpu.CompilerParams(vmem_limit_bytes=8 << 20, **more)


def planes_kernel(fuel, heat, kappa, vel_z, vel_y, to_next, to_prev, arrived):
    planes = fuel.shape[0]
    fields = (fuel, heat, kappa, vel_z, vel_y)
    copies = []
    for target, widths, last in ((to_next, befores, True), (to_prev, afters, False)):
        at = 0
        for field, width in zip(fields, widths):
            if width:
                source = field.at[pl.ds(planes - width if last else 0, width)]
                copies.append((source, target.at[pl.ds(at, width)]))
            at += width
    copies = [
        pltpu.make_async_copy(source, target, arrived.at[i])
        for i, (source, target) in enumerate(copies)
    ]
    for copy in copies:
        copy.start()
    for copy in copies:
        copy.wait()


def deep_planes(fields, low, high):
    planes = fields[0].shape[0]
    at_low = at_high = 0
    columns = []
    for field, before, after, deep in zip(fields, befores, afters, depths):
        column = [(low, at_low + i) for i in range(before)]
        column += [(field, i) for i in range(planes)]
        column += [(high, at_high + i) for i in range(after)]
        last = len(column) - 1
        columns.append(
            [(*plane, 1 + min(deep, j, last - j)) for j, plane in enumerate(column)]
        )
        at_low, at_high = at_low + before, at_high + after
    return columns


def rows_kernel(fuel, heat, kappa, vel_z, vel_y, low, high, outer, inner):
    rows = fuel.shape[1]
    columns = deep_planes((fuel, heat, kappa, vel_z, vel_y), low, high)

    def fill(to_next, to_prev):
        at = 0
        for column in columns:
            for source, i, width in column:
                to_next[at : at + width] = source[i, rows - width : rows]
                to_prev[at : at + width] = source[i, 0:width]
                at += width

    odd = second_core()
    pl.when(odd)(lambda: fill(outer, inner))
    pl.when(jnp.logical_not(odd))(lambda: fill(inner, outer))


def neighbours(blocks, m, lane, rolled):
    def turned(i, by):
        if not 0 <= i < len(blocks):
            return 0.0
        if (i, by) not in rolled:
            rolled[i, by] = pltpu.roll(blocks[i], by, 1)
        return rolled[i, by]

    right = jnp.where(lane < 127, turned(m, 127), turned(m + 1, 127))
    return right + jnp.where(lane > 0, turned(m, 1), turned(m - 1, 1))


def parts(centre, ahead, behind, beside, half_z, half_y):
    up, down = pltpu.roll(centre, centre.shape[0] - 1, 0), pltpu.roll(centre, 1, 0)
    near = (ahead + behind) + (up + down) + beside
    return near - 6.0 * centre, half_z * (ahead - behind) + half_y * (up - down)


def rates(fuels, heats, kappa, vel_z, vel_y):
    half_z, half_y = 0.5 * vel_z, 0.5 * vel_y
    fuel_lap, fuel_adv = parts(*fuels, half_z, half_y)
    heat_lap, heat_adv = parts(*heats, half_z, half_y)
    square = heats[0] * heats[0]
    burning = burn_rate * fuels[0] * square / (1.0 + square)
    return (
        lewis_ratio * kappa * fuel_lap - fuel_adv - burning,
        kappa * heat_lap - heat_adv + heat_release * burning,
    )


def block_transpose(tiles):
    shape = (8, 128)
    row = lax.broadcasted_iota(jnp.int32, shape, 0)
    block = lax.broadcasted_iota(jnp.int32, shape, 1) // 16
    for bit in (4, 2, 1):
        row_bit, block_bit = (row & bit) != 0, (block & bit) != 0
        if bit == 4:
            moved = [pltpu.roll(pltpu.roll(tile, 64, 1), 4, 0) for tile in tiles]
        else:
            right = [pltpu.roll(tile, 16 * bit, 1) for tile in tiles]
            left = [pltpu.roll(tile, 128 - 16 * bit, 1) for tile in tiles]
            right = [pltpu.roll(tile, 8 - bit, 0) for tile in right]
            left = [pltpu.roll(tile, bit, 0) for tile in left]
            moved = [jnp.where(block_bit, r, l) for r, l in zip(right, left)]
        same = row_bit == block_bit
        tiles = [jnp.where(same, tile, other) for tile, other in zip(tiles, moved)]
    return tiles


def step_kernel(
    fuel, heat, kappa, vel_z, vel_y, low, high, outer, inner, out,
    halo, fuel_one, heat_one, heat_two, fuel_two, edge,
):
    planes, rows, size = fuel.shape
    columns = deep_planes((fuel, heat, kappa, vel_z, vel_y), low, high)

    def border(row_low, row_high):
        at = 0
        for j, (source, i, width) in enumerate(sum(columns, [])):
            halo[j, rows - width : rows] = row_low[at : at + width]
            halo[j, 0:width] = row_high[at : at + width]
            at += width

    odd = second_core()
    pl.when(odd)(lambda: border(inner, outer))
    pl.when(jnp.logical_not(odd))(lambda: border(outer, inner))

    parts_of = [slice(at, at + 128) for at in range(0, size, 128)]
    lane = lax.broadcasted_iota(jnp.int32, (2 * rows, 128), 1)

    def plane(field, j, m):
        source, i, width = columns[field][j]
        row = sum(len(column) for column in columns[:field]) + j
        return jnp.concatenate([source[i, :, parts_of[m]], halo[row, :, parts_of[m]]], axis=0)

    coupled = jnp.where(lax.axis_index("depth") > 0, 1.0, 0.0)

    for j in range(planes + 2):
        blocks = [[plane(f, j + 1, m) for m in range(len(parts_of))] for f in (0, 1)]
        rolled = ({}, {})
        for m, part in enumerate(parts_of):
            fuels, heats = (
                (
                    blocks[f][m],
                    plane(f, j + 2, m) * (coupled if j == 1 else 1.0),
                    plane(f, j, m) * (coupled if j == 2 else 1.0),
                    neighbours(blocks[f], m, lane, rolled[f]),
                )
                for f in (0, 1)
            )
            rate_fuel, rate_heat = rates(fuels, heats, *(plane(f, j, m) for f in (2, 3, 4)))
            fuel_one[j, :, part] = fuels[0] + time_step * rate_fuel
            heat_one[j, :, part] = heats[0] + time_step * rate_heat

    for j in range(planes):
        ones = (fuel_one, heat_one)
        blocks = [[ref[j + 1, :, part] for part in parts_of] for ref in ones]
        rolled = ({}, {})
        for m, part in enumerate(parts_of):
            fuels, heats = (
                (
                    blocks[f][m],
                    ones[f][j + 2, :, part] * (coupled if j == 0 else 1.0),
                    ones[f][j, :, part] * (coupled if j == 1 else 1.0),
                    neighbours(blocks[f], m, lane, rolled[f]),
                )
                for f in (0, 1)
            )
            rate_fuel, rate_heat = rates(fuels, heats, *(plane(f, j + 1, m) for f in (2, 3, 4)))
            final = 0.5 * (plane(0, j + 2, m) + fuels[0] + time_step * rate_fuel)
            fuel_two[j, :, part] = final[:rows]
            heat_two[j, :, part] = 0.5 * (plane(1, j + 2, m) + heats[0] + time_step * rate_heat)

    chunk = 2 * planes + 2
    count = size // 16

    def send(values, at):
        groups = size // 128
        tiles = [value[:, m * 128 : (m + 1) * 128] for value in values for m in range(groups)]
        for i, tile in enumerate(block_transpose(tiles)):
            row, m = at + i // groups, i % groups
            place = (8 * m - first_member(count)) % count
            before = min(8, count - place)
            out[pl.ds(place * chunk + row, before, stride=chunk), :] = tile[:before]
            if before < 8:
                out[pl.ds(row, 8 - before, stride=chunk), :] = tile[before:]

    lane = lax.broadcasted_iota(jnp.int32, (rows, size), 1)
    place = lane % 16
    borders = jnp.zeros((rows, size), jnp.float32)
    for p in range(planes):
        level = heat_two[p, :rows]
        send([level], p)
        send([fuel_two[p]], planes + p)
        edge[p : p + 1] = heat_two[p, 2 * rows - 1 : 2 * rows]
        edge[planes + p : planes + p + 1] = heat_two[p, rows : rows + 1]
        left = (place == p) & (lane >= 16)
        right = (place == planes + p) & (lane < size - 16)
        borders = jnp.where(left, pltpu.roll(level, p + 1, 1), borders)
        borders = jnp.where(right, pltpu.roll(level, size - 16 + planes + p, 1), borders)
    send([edge[...]], 2 * planes)
    send([borders], 2 * planes + 1)


def per_function(ref, *index):
    row = lax.broadcasted_iota(jnp.int32, (8, 128), 0)
    value = jnp.full((8, 128), ref[(0,) + index], jnp.float32)
    for k in range(1, 8):
        value = jnp.where(row == k, ref[(k,) + index], value)
    return value


def functions_kernel(opacity_scale, centre, width, density, tint, out):
    spread = per_function(width)
    out[0] = per_function(centre)
    out[1] = -log2_e / (spread * spread)
    out[2] = per_function(density) * (-log2_e * opacity_scale)
    for c in range(3):
        out[3 + c] = 0.5 * per_function(tint, c)


def march_kernel(planes, functions, fields, out, lights):
    chunk = 2 * planes + 2
    count = fields.shape[0] // chunk
    columns = [fields[pl.ds(i, count, stride=chunk), :] for i in range(planes)]
    edge, borders = (
        fields[pl.ds(2 * planes + i, count, stride=chunk), :] for i in range(2)
    )
    lane = lax.broadcasted_iota(jnp.int32, (count, 128), 1)
    place = lane % 16
    row = lax.broadcasted_iota(jnp.int32, (count, 128), 0)
    coupled = row != (count - first_member(count)) % count
    for p in range(planes):
        level = columns[p]
        ahead = columns[p + 1] if p + 1 < planes else pltpu.roll(columns[0], count - 1, 0)
        behind = columns[p - 1] if p > 0 else pltpu.roll(columns[planes - 1], 1, 0)
        if p == 0:
            ahead = jnp.where(coupled, ahead, 0.0)
        if p == 1:
            behind = jnp.where(coupled, behind, 0.0)

        def moved(value, by):
            by = by % 128
            return pltpu.roll(value, by, 1) if by else value

        up = jnp.where(lane < 112, moved(level, -16), moved(edge, 112 - 16 * (planes + p)))
        down = jnp.where(lane >= 16, moved(level, 16), moved(edge, -16 * p))
        right = jnp.where(place < 15, moved(level, -1), moved(borders, 15 - planes - p))
        left = jnp.where(place > 0, moved(level, 1), moved(borders, -p))
        grad_z, grad_y, grad_x = 0.5 * (ahead - behind), 0.5 * (up - down), 0.5 * (right - left)
        norm_sq = grad_z * grad_z + grad_y * grad_y + grad_x * grad_x + 1.0
        facing = 0.48 * grad_z + 0.6 * grad_y + 0.64 * grad_x
        lights[p] = 0.5 * (0.35 + 0.65 * (facing * facing) / norm_sq)

    mid, narrow, thick, *half = (functions[i] for i in range(6))

    def one_plane(at, s, p, state):
        passing, total, *colour = state
        level, fuel = fields[pl.ds(at + p, 1), :], fields[pl.ds(at + planes + p, 1), :]
        offset = level - mid
        survive = jnp.exp2(thick * jnp.exp2(narrow * (offset * offset)))
        left = passing * survive
        weight = (passing - left) * lights[p, pl.ds(s, 1)]
        colour = [value + weight * jnp.tanh(half[c] * fuel) for c, value in enumerate(colour)]
        return (left, total + weight, *colour)

    joint = 16

    def segments(i, state):
        for s in range(joint):
            s = i * joint + s + (count - first_member(count))
            now, after = lax.rem(s, count), lax.rem(s + 1, count)
            for p in range(1, planes):
                state = one_plane(now * chunk, now, p, state)
            state = one_plane(after * chunk, after, 0, state)
        return state

    zero = jnp.zeros((8, 128), jnp.float32)
    state = lax.fori_loop(0, count // joint, segments, (zero + 1.0, zero, zero, zero, zero))
    passing, total, *colour = state
    values = [total + value for value in colour] + [passing]
    for c, tile in enumerate(block_transpose(values)):
        for k in range(8):
            out[k, c] = tile[:, 16 * k : 16 * k + 16]


def body(fuel, heat, kappa, vel_z, vel_y, tf_centre, tf_width, tf_density, tf_tint):
    planes, rows, columns = fuel.shape
    depth_count = lax.axis_size("depth")
    fields = (fuel, heat, kappa, vel_z, vel_y)
    f32 = functools.partial(jax.ShapeDtypeStruct, dtype=jnp.float32)
    sent_rows = sum(planes * (1 + deep) + deep * (1 + deep) for deep in depths)

    to_next, to_prev = pl.pallas_call(
        planes_kernel,
        out_shape=[f32((sum(widths), rows, columns)) for widths in (befores, afters)],
        in_specs=[hbm] * 5,
        out_specs=[vmem] * 2,
        scratch_shapes=[pltpu.SemaphoreType.DMA((2 * len(depths),))],
        compiler_params=params(),
        name="pack_planes",
    )(*(pltpu.with_memory_space_constraint(field, pltpu.HBM) for field in fields))
    low, high = exchange(to_next, to_prev, "depth")
    outer, inner = pl.pallas_call(
        rows_kernel,
        out_shape=[f32((sent_rows, columns))] * 2,
        in_specs=[vmem] * 7,
        out_specs=[vmem] * 2,
        compiler_params=params(),
        name="pack_rows",
    )(*fields, low, high)
    outer, inner = swap(outer, "rows", 1), swap(inner, "rows", 0)

    chunk = 2 * planes + 2
    tall = 2 * rows
    deep_count = sum(planes + 2 * deep for deep in depths)
    scratch = [pltpu.VMEM((deep_count, rows, columns), jnp.float32)]
    scratch += [pltpu.VMEM((planes + 2, tall, columns), jnp.float32)] * 2
    scratch += [pltpu.VMEM((planes, tall, columns), jnp.float32)]
    scratch += [pltpu.VMEM((planes, rows, columns), jnp.float32)]
    scratch += [pltpu.VMEM((2 * planes, columns), jnp.float32)]
    stepped = pl.pallas_call(
        step_kernel,
        out_shape=f32((depth_count * chunk, 128)),
        in_specs=[vmem] * 9,
        out_specs=vmem,
        scratch_shapes=scratch,
        compiler_params=params(),
        name="step",
    )(*fields, low, high, outer, inner)

    order = [(first_member(depth_count) + i) % depth_count for i in range(depth_count)]
    gathered = lax.all_to_all(
        stepped.reshape(depth_count, 1, chunk * 128),
        "depth",
        split_axis=0,
        concat_axis=0,
        axis_index_groups=[order],
        tiled=True,
    ).reshape(depth_count * chunk, 128)

    functions = pl.pallas_call(
        functools.partial(functions_kernel, 4.0 / (planes * depth_count)),
        out_shape=f32((6, 8, 128)),
        in_specs=[smem] * 4,
        out_specs=vmem,
        compiler_params=params(),
        name="functions",
    )(tf_centre, tf_width, tf_density, tf_tint)

    return pl.pallas_call(
        functools.partial(march_kernel, planes),
        out_shape=f32((8, 4, rows, columns // depth_count)),
        in_specs=[vmem] * 2,
        out_specs=vmem,
        scratch_shapes=[pltpu.VMEM((planes, depth_count, 128), jnp.float32)],
        compiler_params=params(),
        name="march",
    )(functions, gathered)


def solution(mesh):
    placed = (P("depth", "rows", None),) * 5 + (P(),) * 4
    return jax.shard_map(
        body, mesh=mesh, in_specs=placed, out_specs=P(None, None, "rows", "depth"), check_vma=False
    )
```

```python
import functools
import math

import jax
import jax.numpy as jnp
from jax import lax
from jax.experimental import pallas as pl
from jax.experimental.pallas import tpu as pltpu
from jax.sharding import PartitionSpec as P

time_step = 1.0
lewis_ratio = 0.8
heat_release = 0.6
burn_rate = 0.5

befores = (3, 3, 2, 2, 2)
afters = (1, 1, 0, 0, 0)
depths = (2, 2, 1, 1, 1)
log2_e = math.log2(math.e)

vmem = pl.BlockSpec(memory_space=pltpu.VMEM)
smem = pl.BlockSpec(memory_space=pltpu.SMEM)
hbm = pl.BlockSpec(memory_space=pltpu.HBM)


def first_member(count):
    return 11 * count // 16


def exchange(to_next, to_prev, axis):
    count = lax.axis_size(axis)
    forward = [(i, (i + 1) % count) for i in range(count)]
    backward = [(i + 1, i) for i in range(count - 1)]
    return lax.ppermute(to_next, axis, forward), lax.ppermute(to_prev, axis, backward)


def swap(block, axis, first):
    count = lax.axis_size(axis)
    forward = [(i, i + 1) for i in range(first, count - 1, 2)]
    return lax.ppermute(block, axis, forward + [(target, source) for source, target in forward])


def second_core():
    return lax.rem(lax.axis_index("rows"), 2) == 1


def params(**more):
    return pltpu.CompilerParams(vmem_limit_bytes=8 << 20, **more)


def planes_kernel(fuel, heat, kappa, vel_z, vel_y, to_next, to_prev, arrived):
    planes = fuel.shape[0]
    fields = (fuel, heat, kappa, vel_z, vel_y)
    copies = []
    for target, widths, last in ((to_next, befores, True), (to_prev, afters, False)):
        at = 0
        for field, width in zip(fields, widths):
            if width:
                source = field.at[pl.ds(planes - width if last else 0, width)]
                copies.append((source, target.at[pl.ds(at, width)]))
            at += width
    copies = [
        pltpu.make_async_copy(source, target, arrived.at[i])
        for i, (source, target) in enumerate(copies)
    ]
    for copy in copies:
        copy.start()
    for copy in copies:
        copy.wait()


def deep_planes(fields, low, high):
    planes = fields[0].shape[0]
    at_low = at_high = 0
    columns = []
    for field, before, after, deep in zip(fields, befores, afters, depths):
        column = [(low, at_low + i) for i in range(before)]
        column += [(field, i) for i in range(planes)]
        column += [(high, at_high + i) for i in range(after)]
        last = len(column) - 1
        columns.append(
            [(*plane, 1 + min(deep, j, last - j)) for j, plane in enumerate(column)]
        )
        at_low, at_high = at_low + before, at_high + after
    return columns


def rows_kernel(fuel, heat, kappa, vel_z, vel_y, low, high, outer, inner):
    rows = fuel.shape[1]
    columns = deep_planes((fuel, heat, kappa, vel_z, vel_y), low, high)

    def fill(to_next, to_prev):
        at = 0
        for column in columns:
            for source, i, width in column:
                to_next[at : at + width] = source[i, rows - width : rows]
                to_prev[at : at + width] = source[i, 0:width]
                at += width

    odd = second_core()
    pl.when(odd)(lambda: fill(outer, inner))
    pl.when(jnp.logical_not(odd))(lambda: fill(inner, outer))


def neighbours(blocks, m, lane, rolled):
    def turned(i, by):
        if not 0 <= i < len(blocks):
            return 0.0
        if (i, by) not in rolled:
            rolled[i, by] = pltpu.roll(blocks[i], by, 1)
        return rolled[i, by]

    right = jnp.where(lane < 127, turned(m, 127), turned(m + 1, 127))
    return right + jnp.where(lane > 0, turned(m, 1), turned(m - 1, 1))


def parts(centre, ahead, behind, beside, half_z, half_y):
    up, down = pltpu.roll(centre, centre.shape[0] - 1, 0), pltpu.roll(centre, 1, 0)
    near = (ahead + behind) + (up + down) + beside
    return near - 6.0 * centre, half_z * (ahead - behind) + half_y * (up - down)


def rates(fuels, heats, kappa, vel_z, vel_y):
    half_z, half_y = 0.5 * vel_z, 0.5 * vel_y
    fuel_lap, fuel_adv = parts(*fuels, half_z, half_y)
    heat_lap, heat_adv = parts(*heats, half_z, half_y)
    square = heats[0] * heats[0]
    burning = burn_rate * fuels[0] * square / (1.0 + square)
    return (
        lewis_ratio * kappa * fuel_lap - fuel_adv - burning,
        kappa * heat_lap - heat_adv + heat_release * burning,
    )


def block_transpose(tiles):
    shape = (8, 128)
    row = lax.broadcasted_iota(jnp.int32, shape, 0)
    block = lax.broadcasted_iota(jnp.int32, shape, 1) // 16
    for bit in (4, 2, 1):
        row_bit, block_bit = (row & bit) != 0, (block & bit) != 0
        if bit == 4:
            moved = [pltpu.roll(pltpu.roll(tile, 64, 1), 4, 0) for tile in tiles]
        else:
            right = [pltpu.roll(tile, 16 * bit, 1) for tile in tiles]
            left = [pltpu.roll(tile, 128 - 16 * bit, 1) for tile in tiles]
            right = [pltpu.roll(tile, 8 - bit, 0) for tile in right]
            left = [pltpu.roll(tile, bit, 0) for tile in left]
            moved = [jnp.where(block_bit, r, l) for r, l in zip(right, left)]
        same = row_bit == block_bit
        tiles = [jnp.where(same, tile, other) for tile, other in zip(tiles, moved)]
    return tiles


def step_kernel(
    fuel, heat, kappa, vel_z, vel_y, low, high, outer, inner, out,
    halo, fuel_one, heat_one, heat_two, fuel_two, edge,
):
    planes, rows, size = fuel.shape
    columns = deep_planes((fuel, heat, kappa, vel_z, vel_y), low, high)

    def border(row_low, row_high):
        at = 0
        for j, (source, i, width) in enumerate(sum(columns, [])):
            halo[j, rows - width : rows] = row_low[at : at + width]
            halo[j, 0:width] = row_high[at : at + width]
            at += width

    odd = second_core()
    pl.when(odd)(lambda: border(inner, outer))
    pl.when(jnp.logical_not(odd))(lambda: border(outer, inner))

    parts_of = [slice(at, at + 128) for at in range(0, size, 128)]
    lane = lax.broadcasted_iota(jnp.int32, (2 * rows, 128), 1)

    def plane(field, j, m):
        source, i, width = columns[field][j]
        row = sum(len(column) for column in columns[:field]) + j
        return jnp.concatenate([source[i, :, parts_of[m]], halo[row, :, parts_of[m]]], axis=0)

    coupled = jnp.where(lax.axis_index("depth") > 0, 1.0, 0.0)

    for j in range(planes + 2):
        blocks = [[plane(f, j + 1, m) for m in range(len(parts_of))] for f in (0, 1)]
        rolled = ({}, {})
        for m, part in enumerate(parts_of):
            fuels, heats = (
                (
                    blocks[f][m],
                    plane(f, j + 2, m) * (coupled if j == 1 else 1.0),
                    plane(f, j, m) * (coupled if j == 2 else 1.0),
                    neighbours(blocks[f], m, lane, rolled[f]),
                )
                for f in (0, 1)
            )
            rate_fuel, rate_heat = rates(fuels, heats, *(plane(f, j, m) for f in (2, 3, 4)))
            fuel_one[j, :, part] = fuels[0] + time_step * rate_fuel
            heat_one[j, :, part] = heats[0] + time_step * rate_heat

    for j in range(planes):
        ones = (fuel_one, heat_one)
        blocks = [[ref[j + 1, :, part] for part in parts_of] for ref in ones]
        rolled = ({}, {})
        for m, part in enumerate(parts_of):
            fuels, heats = (
                (
                    blocks[f][m],
                    ones[f][j + 2, :, part] * (coupled if j == 0 else 1.0),
                    ones[f][j, :, part] * (coupled if j == 1 else 1.0),
                    neighbours(blocks[f], m, lane, rolled[f]),
                )
                for f in (0, 1)
            )
            rate_fuel, rate_heat = rates(fuels, heats, *(plane(f, j + 1, m) for f in (2, 3, 4)))
            final = 0.5 * (plane(0, j + 2, m) + fuels[0] + time_step * rate_fuel)
            fuel_two[j, :, part] = final[:rows]
            heat_two[j, :, part] = 0.5 * (plane(1, j + 2, m) + heats[0] + time_step * rate_heat)

    chunk = 2 * planes + 2
    count = size // 16

    def send(values, at):
        groups = size // 128
        tiles = [value[:, m * 128 : (m + 1) * 128] for value in values for m in range(groups)]
        for i, tile in enumerate(block_transpose(tiles)):
            row, m = at + i // groups, i % groups
            place = (8 * m - first_member(count)) % count
            before = min(8, count - place)
            out[pl.ds(place * chunk + row, before, stride=chunk), :] = tile[:before]
            if before < 8:
                out[pl.ds(row, 8 - before, stride=chunk), :] = tile[before:]

    lane = lax.broadcasted_iota(jnp.int32, (rows, size), 1)
    place = lane % 16
    borders = jnp.zeros((rows, size), jnp.float32)
    for p in range(planes):
        level = heat_two[p, :rows]
        send([level], p)
        send([fuel_two[p]], planes + p)
        edge[p : p + 1] = heat_two[p, 2 * rows - 1 : 2 * rows]
        edge[planes + p : planes + p + 1] = heat_two[p, rows : rows + 1]
        left = (place == p) & (lane >= 16)
        right = (place == planes + p) & (lane < size - 16)
        borders = jnp.where(left, pltpu.roll(level, p + 1, 1), borders)
        borders = jnp.where(right, pltpu.roll(level, size - 16 + planes + p, 1), borders)
    send([edge[...]], 2 * planes)
    send([borders], 2 * planes + 1)


def per_function(ref, *index):
    row = lax.broadcasted_iota(jnp.int32, (8, 128), 0)
    value = jnp.full((8, 128), ref[(0,) + index], jnp.float32)
    for k in range(1, 8):
        value = jnp.where(row == k, ref[(k,) + index], value)
    return value


def functions_kernel(opacity_scale, centre, width, density, tint, out):
    spread = per_function(width)
    out[0] = per_function(centre)
    out[1] = -log2_e / (spread * spread)
    out[2] = per_function(density) * (-log2_e * opacity_scale)
    for c in range(3):
        out[3 + c] = 0.5 * per_function(tint, c)


def march_kernel(planes, functions, fields, out, lights):
    chunk = 2 * planes + 2
    count = fields.shape[0] // chunk
    columns = [fields[pl.ds(i, count, stride=chunk), :] for i in range(planes)]
    edge, borders = (
        fields[pl.ds(2 * planes + i, count, stride=chunk), :] for i in range(2)
    )
    lane = lax.broadcasted_iota(jnp.int32, (count, 128), 1)
    place = lane % 16
    row = lax.broadcasted_iota(jnp.int32, (count, 128), 0)
    coupled = row != (count - first_member(count)) % count
    for p in range(planes):
        level = columns[p]
        ahead = columns[p + 1] if p + 1 < planes else pltpu.roll(columns[0], count - 1, 0)
        behind = columns[p - 1] if p > 0 else pltpu.roll(columns[planes - 1], 1, 0)
        if p == 0:
            ahead = jnp.where(coupled, ahead, 0.0)
        if p == 1:
            behind = jnp.where(coupled, behind, 0.0)

        def moved(value, by):
            by = by % 128
            return pltpu.roll(value, by, 1) if by else value

        up = jnp.where(lane < 112, moved(level, -16), moved(edge, 112 - 16 * (planes + p)))
        down = jnp.where(lane >= 16, moved(level, 16), moved(edge, -16 * p))
        right = jnp.where(place < 15, moved(level, -1), moved(borders, 15 - planes - p))
        left = jnp.where(place > 0, moved(level, 1), moved(borders, -p))
        grad_z, grad_y, grad_x = 0.5 * (ahead - behind), 0.5 * (up - down), 0.5 * (right - left)
        norm_sq = grad_z * grad_z + grad_y * grad_y + grad_x * grad_x + 1.0
        facing = 0.48 * grad_z + 0.6 * grad_y + 0.64 * grad_x
        lights[p] = 0.5 * (0.35 + 0.65 * (facing * facing) / norm_sq)

    mid, narrow, thick, *half = (functions[i] for i in range(6))

    def one_plane(at, s, p, state):
        passing, total, *colour = state
        level, fuel = fields[pl.ds(at + p, 1), :], fields[pl.ds(at + planes + p, 1), :]
        offset = level - mid
        survive = jnp.exp2(thick * jnp.exp2(narrow * (offset * offset)))
        left = passing * survive
        weight = (passing - left) * lights[p, pl.ds(s, 1)]
        colour = [value + weight * jnp.tanh(half[c] * fuel) for c, value in enumerate(colour)]
        return (left, total + weight, *colour)

    joint = 16

    def segments(i, state):
        for s in range(joint):
            s = i * joint + s + (count - first_member(count))
            now, after = lax.rem(s, count), lax.rem(s + 1, count)
            for p in range(1, planes):
                state = one_plane(now * chunk, now, p, state)
            state = one_plane(after * chunk, after, 0, state)
        return state

    zero = jnp.zeros((8, 128), jnp.float32)
    state = lax.fori_loop(0, count // joint, segments, (zero + 1.0, zero, zero, zero, zero))
    passing, total, *colour = state
    values = [total + value for value in colour] + [passing]
    for c, tile in enumerate(block_transpose(values)):
        for k in range(8):
            out[k, c] = tile[:, 16 * k : 16 * k + 16]


def body(fuel, heat, kappa, vel_z, vel_y, tf_centre, tf_width, tf_density, tf_tint):
    planes, rows, columns = fuel.shape
    depth_count = lax.axis_size("depth")
    fields = (fuel, heat, kappa, vel_z, vel_y)
    f32 = functools.partial(jax.ShapeDtypeStruct, dtype=jnp.float32)
    sent_rows = sum(planes * (1 + deep) + deep * (1 + deep) for deep in depths)

    to_next, to_prev = pl.pallas_call(
        planes_kernel,
        out_shape=[f32((sum(widths), rows, columns)) for widths in (befores, afters)],
        in_specs=[hbm] * 5,
        out_specs=[vmem] * 2,
        scratch_shapes=[pltpu.SemaphoreType.DMA((2 * len(depths),))],
        compiler_params=params(),
        name="pack_planes",
    )(*(pltpu.with_memory_space_constraint(field, pltpu.HBM) for field in fields))
    low, high = exchange(to_next, to_prev, "depth")
    outer, inner = pl.pallas_call(
        rows_kernel,
        out_shape=[f32((sent_rows, columns))] * 2,
        in_specs=[vmem] * 7,
        out_specs=[vmem] * 2,
        compiler_params=params(),
        name="pack_rows",
    )(*fields, low, high)
    outer, inner = swap(outer, "rows", 1), swap(inner, "rows", 0)

    chunk = 2 * planes + 2
    tall = 2 * rows
    deep_count = sum(planes + 2 * deep for deep in depths)
    scratch = [pltpu.VMEM((deep_count, rows, columns), jnp.float32)]
    scratch += [pltpu.VMEM((planes + 2, tall, columns), jnp.float32)] * 2
    scratch += [pltpu.VMEM((planes, tall, columns), jnp.float32)]
    scratch += [pltpu.VMEM((planes, rows, columns), jnp.float32)]
    scratch += [pltpu.VMEM((2 * planes, columns), jnp.float32)]
    stepped = pl.pallas_call(
        step_kernel,
        out_shape=f32((depth_count * chunk, 128)),
        in_specs=[vmem] * 9,
        out_specs=vmem,
        scratch_shapes=scratch,
        compiler_params=params(),
        name="step",
    )(*fields, low, high, outer, inner)

    order = [(first_member(depth_count) + i) % depth_count for i in range(depth_count)]
    gathered = lax.all_to_all(
        stepped.reshape(depth_count, 1, chunk * 128),
        "depth",
        split_axis=0,
        concat_axis=0,
        axis_index_groups=[order],
        tiled=True,
    ).reshape(depth_count * chunk, 128)

    functions = pl.pallas_call(
        functools.partial(functions_kernel, 4.0 / (planes * depth_count)),
        out_shape=f32((6, 8, 128)),
        in_specs=[smem] * 4,
        out_specs=vmem,
        compiler_params=params(),
        name="functions",
    )(tf_centre, tf_width, tf_density, tf_tint)

    return pl.pallas_call(
        functools.partial(march_kernel, planes),
        out_shape=f32((8, 4, rows, columns // depth_count)),
        in_specs=[vmem] * 2,
        out_specs=vmem,
        scratch_shapes=[pltpu.VMEM((planes, depth_count, 128), jnp.float32)],
        compiler_params=params(),
        name="march",
    )(functions, gathered)


def solution(mesh):
    placed = (P("depth", "rows", None),) * 5 + (P(),) * 4
    return jax.shard_map(
        body, mesh=mesh, in_specs=placed, out_specs=P(None, None, "rows", "depth"), check_vma=False
    )
```
